32 devices in a mesh: pts: 8 (over z, core), head: 4 (over y, x).
Axes of the slice: x: 2, y: 2, z: 4, core: 2. Of those that a mesh axis runs over, the one named last changes fastest.
Arguments:
- mesh_signals: bfloat16 [262144, 256], P('pts'), may hold values from -7 to 7
- loss_sensitivity: bfloat16 [262144, 256], P(('pts', 'head')), may hold values from -0.01171875 to 0.01171875
- divider_projection: bfloat16 [256, 256], P(None, 'head'), may hold values from -0.375 to 0.375
- partition_projection: bfloat16 [256, 256], P(None, 'head'), may hold values from -0.375 to 0.375
- sharpness_axis: float32 [256], P('head'), may hold values from -4 to 4
- partition_energies: float32 [8, 32, 64], P('head'), may hold values from -6 to 6
- asking_projection: float32 [8, 32, 32], P('head'), may hold values from -6 to 6
- lookup_projection: float32 [8, 32, 32], P('head'), may hold values from -6 to 6
- content_projection: float32 [8, 32, 32], P('head'), may hold values from -1 to 1
- prefocus_scale: float32 [256], replicated, may hold values from 0.1 to 1.9
- emit_projection: bfloat16 [256, 256], replicated, may hold values from -0.375 to 0.375
- premlp_scale: float32 [256], replicated, may hold values from 0.1 to 1.9
- expand_factor: bfloat16 [256, 256], replicated, may hold values from -0.375 to 0.375
- expand_offset: float32 [256], replicated, may hold values from -3 to 3
- contract_factor: bfloat16 [256, 256], replicated, may hold values from -0.375 to 0.375
Outputs:
- block_result: bfloat16 [262144, 256], P(('pts', 'head'))
- divider_proj_slope: float32 [256, 256], P(None, 'head')
- partition_proj_slope: float32 [256, 256], P(None, 'head')
- sharpness_axis_slope: float32 [256], P('head')
- partition_energy_slope: float32 [8, 32, 64], P('head')
- asking_proj_slope: float32 [8, 32, 32], P('head')
- lookup_proj_slope: float32 [8, 32, 32], P('head')
- content_proj_slope: float32 [8, 32, 32], P('head')
- prefocus_scale_slope: float32 [256], replicated
- emit_proj_slope: float32 [256, 256], replicated
- premlp_scale_slope: float32 [256], replicated
- expand_factor_slope: float32 [256, 256], replicated
- expand_offset_slope: float32 [256], replicated
- contract_factor_slope: float32 [256, 256], replicated
The draws below stay inside these ranges and needn't reach their ends.
All inputs are finite; a program needn't handle non-finite values.
Results may differ from the reference program's by a relative error of at most 0.011.
Values may be sent and summed in bfloat16 or wider, within the bound.
No kernel may reach another device: no remote copies, remote signals or barrier semaphores. Data moves between devices by JAX's collectives and lax.ppermute only.
A program may use at most 256 MiB of HBM per device.

```python
import math
import jax
import jax.numpy as jnp
from jax import lax

HEADS = 8
HEAD_DIM = 32
SLICES = 64
FF = 256
EMBED_SIZE = 256
PTS_DEV = 32768
POINTS = 262144
N_PTS = 8


def draw_mesh_signals(key, part):
    wave_key, phase_key, height_key, noise_key = jax.random.split(key, 4)
    position = jnp.arange(POINTS, dtype=jnp.float32) / POINTS
    wave_count = jax.random.randint(wave_key, (EMBED_SIZE,), 1, 5).astype(jnp.float32)
    phase_shift = jax.random.uniform(phase_key, (EMBED_SIZE,), jnp.float32, -math.pi, math.pi)
    height = jax.random.uniform(height_key, (EMBED_SIZE,), jnp.float32, 0.8, 2.0)
    noise_part = jax.random.truncated_normal(noise_key, -4.0, 4.0, (POINTS, EMBED_SIZE), jnp.float32)
    smooth = height * jnp.sin(2.0 * math.pi * wave_count * position[:, None] + phase_shift)
    return (noise_part + smooth).astype(jnp.bfloat16)


def level_of(rng, shape, pieces, smallest, high):
    factor_of = 1.0
    for dim, blocks in pieces:
        steps = jax.random.uniform(jax.random.fold_in(jax.random.fold_in(rng, 6), dim), (blocks,), jnp.float32, smallest / len(pieces), high / len(pieces))
        factor_of = factor_of * jnp.repeat(jnp.exp(steps), shape[dim] // blocks).reshape((-1,) + (1,) * (len(shape) - 1 - dim))
    return factor_of


def gaussian(rng, shape, scale, reach, cuts=(), kind=jnp.bfloat16):
    result = scale * jax.random.normal(rng, shape, jnp.float32)
    if cuts:
        result = result * level_of(rng, shape, cuts, -0.22, 0.18)
    return jnp.clip(result, -reach, reach).astype(kind)


def setup_inputs(seed: int = 0) -> dict:
    keys = jax.random.split(jax.random.key(seed), 16)
    mesh_signals = draw_mesh_signals(jax.random.fold_in(keys[15], 71), 0)
    loss_sensitivity = gaussian(keys[1], (POINTS, EMBED_SIZE), POINTS ** -0.5, 0.01171875, ((0, 32),))
    divider_projection = gaussian(keys[2], (EMBED_SIZE, EMBED_SIZE), EMBED_SIZE ** -0.5, 0.375, ((1, 4),))
    partition_projection = gaussian(keys[3], (EMBED_SIZE, EMBED_SIZE), EMBED_SIZE ** -0.5, 0.375, ((1, 4),))
    sharpness_axis = gaussian(keys[4], (EMBED_SIZE,), 0.25, 4.0, ((0, 4),), jnp.float32)
    partition_energies = gaussian(keys[5], (HEADS, HEAD_DIM, SLICES), 0.5, 6.0, ((0, 4),), jnp.float32)
    asking_projection = gaussian(keys[6], (HEADS, HEAD_DIM, HEAD_DIM), 0.5, 6.0, ((0, 4),), jnp.float32)
    lookup_projection = gaussian(keys[7], (HEADS, HEAD_DIM, HEAD_DIM), 0.5, 6.0, ((0, 4),), jnp.float32)
    content_projection = gaussian(keys[8], (HEADS, HEAD_DIM, HEAD_DIM), HEAD_DIM ** -0.5, 1.0, ((0, 4),), jnp.float32)
    prefocus_scale = jnp.clip(1.0 + 0.18 * jax.random.normal(keys[9], (EMBED_SIZE,), jnp.float32), 0.1, 1.9)
    emit_projection = gaussian(keys[10], (EMBED_SIZE, EMBED_SIZE), EMBED_SIZE ** -0.5, 0.375)
    premlp_scale = jnp.clip(1.0 + 0.18 * jax.random.normal(keys[11], (EMBED_SIZE,), jnp.float32), 0.1, 1.9)
    expand_factor = gaussian(keys[12], (EMBED_SIZE, FF), EMBED_SIZE ** -0.5, 0.375)
    expand_offset = gaussian(keys[13], (FF,), 0.5, 3.0, (), jnp.float32)
    contract_factor = gaussian(keys[14], (FF, EMBED_SIZE), FF ** -0.5, 0.375)
    return {"mesh_signals": mesh_signals, "loss_sensitivity": loss_sensitivity, "divider_projection": divider_projection, "partition_projection": partition_projection, "sharpness_axis": sharpness_axis, "partition_energies": partition_energies, "asking_projection": asking_projection, "lookup_projection": lookup_projection, "content_projection": content_projection, "prefocus_scale": prefocus_scale, "emit_projection": emit_projection, "premlp_scale": premlp_scale, "expand_factor": expand_factor, "expand_offset": expand_offset, "contract_factor": contract_factor}


SCORE_LIMIT = 30.0
NORM_EPS = 1e-05

def product_f32(form, left_side, right_side):
    return jnp.einsum(form, left_side.astype(jnp.float32), right_side.astype(jnp.float32), precision=lax.Precision.HIGHEST)

def matmul_f32(left_side, right_side):
    return jnp.dot(left_side.astype(jnp.float32), right_side.astype(jnp.float32), precision=lax.Precision.HIGHEST)

def layer_rows(values):
    values = values.astype(jnp.float32)
    centered = values - lax.optimization_barrier(jnp.mean(values, axis=-1, keepdims=True))
    spread = lax.optimization_barrier(jnp.mean(centered * centered, axis=-1, keepdims=True))
    return centered * lax.rsqrt(spread + NORM_EPS)

def scale_rows(values, gain):
    return layer_rows(values) * gain

def partition_membership(interior_signals, partition_energies, sharpness_branches):
    partition_sharpness = 0.5 + jax.nn.softplus(jnp.einsum('cz,czq->cq', sharpness_branches, interior_signals, precision=lax.Precision.HIGHEST))
    partition_energy = jnp.einsum('hes,hem->hsm', partition_energies, interior_signals, precision=lax.Precision.HIGHEST)
    bounded_energies = SCORE_LIMIT * jnp.tanh(partition_energy / (SCORE_LIMIT * partition_sharpness[:, None, :]))
    raised = jnp.exp(bounded_energies)
    return raised / lax.optimization_barrier(jnp.sum(raised, axis=1, keepdims=True))

def token_attention(total_num, total_den, asking_projection, lookup_projection, content_projection):
    tokens = total_num / (total_den[:, :, None] + NORM_EPS)
    query_rows = jnp.einsum('hse,hef->hsf', tokens, asking_projection, precision=lax.Precision.HIGHEST)
    key_rows = jnp.einsum('hse,hef->hsf', tokens, lookup_projection, precision=lax.Precision.HIGHEST)
    value_rows = jnp.einsum('hse,hef->hsf', tokens, content_projection, precision=lax.Precision.HIGHEST)
    scores = jnp.einsum('hsf,htf->hst', query_rows, key_rows, precision=lax.Precision.HIGHEST) * query_rows.shape[-1] ** (-0.5)
    bounded_energies = SCORE_LIMIT * jnp.tanh(scores / SCORE_LIMIT)
    raised = jnp.exp(bounded_energies)
    attend = raised / lax.optimization_barrier(jnp.sum(raised, axis=-1, keepdims=True))
    return jnp.einsum('hst,htf->hsf', attend, value_rows, precision=lax.Precision.HIGHEST)

def focus_evaluate(entering_samples, prefocus_scale, divider_projection, partition_projection, sharpness_axis, partition_energies):
    number_branches, branch_breadth, slice_count = partition_energies.shape
    row_count = entering_samples.shape[0]
    normal_rows = layer_rows(entering_samples)
    scaled_low = (normal_rows * prefocus_scale).astype(jnp.bfloat16)
    interior_signals = matmul_f32(scaled_low, divider_projection).T.reshape(number_branches, branch_breadth, row_count)
    feat_full = matmul_f32(scaled_low, partition_projection)
    feat_low = feat_full.astype(jnp.bfloat16).T.reshape(number_branches, branch_breadth, row_count)
    parameter_nest, partition_reverse = jax.vjp(partition_membership, interior_signals, partition_energies, sharpness_axis.reshape(number_branches, branch_breadth))
    weights_low = parameter_nest.astype(jnp.bfloat16)
    part_num = product_f32('hsm,hem->hse', weights_low, feat_low)
    part_den = lax.optimization_barrier(jnp.sum(parameter_nest, axis=2))
    return (normal_rows, feat_low, weights_low, partition_reverse, part_num, part_den)

def deslice_heads(weights_low, token_low):
    number_branches, slice_count, branch_breadth = token_low.shape
    mixed = product_f32('hsm,hse->hem', weights_low, token_low)
    return mixed.reshape(number_branches * branch_breadth, weights_low.shape[2]).astype(jnp.bfloat16)

def token_gradient(weights_low, back_mixed):
    number_branches, slice_count, row_count = weights_low.shape
    back_heads = back_mixed.reshape(number_branches, back_mixed.shape[0] // number_branches, row_count)
    return product_f32('hsm,hem->hse', weights_low, back_heads)

def mixer_pass(mixed_rows, own_rows, loss_sensitivity, emit_projection, premlp_scale, expand_factor, expand_offset, contract_factor):
    attended = matmul_f32(mixed_rows.T, emit_projection)
    residual = own_rows.astype(jnp.float32) + attended
    normed, norm_backward = jax.vjp(scale_rows, residual, premlp_scale)
    normed_low = normed.astype(jnp.bfloat16)
    inner_act = matmul_f32(normed_low, expand_factor) + expand_offset
    active, gelu_backward = jax.vjp(jax.nn.gelu, inner_act)
    active_low = active.astype(jnp.bfloat16)
    block_result = (residual + matmul_f32(active_low, contract_factor)).astype(jnp.bfloat16)
    contract_factor_slope = matmul_f32(active_low.T, loss_sensitivity)
    back_active = matmul_f32(loss_sensitivity, contract_factor.T)
    back_inner, = gelu_backward(back_active)
    back_inner_low = back_inner.astype(jnp.bfloat16)
    expand_factor_slope = matmul_f32(normed_low.T, back_inner_low)
    grad_bias = lax.optimization_barrier(jnp.sum(back_inner, axis=0))
    back_normed = matmul_f32(back_inner_low, expand_factor.T)
    back_norm_resid, grad_gain = norm_backward(back_normed)
    back_resid_low = (loss_sensitivity.astype(jnp.float32) + back_norm_resid).astype(jnp.bfloat16)
    emit_proj_slope = matmul_f32(mixed_rows, back_resid_low)
    back_mixed = matmul_f32(emit_projection, back_resid_low.T).astype(jnp.bfloat16)
    return (block_result, back_mixed, (emit_proj_slope, grad_gain, expand_factor_slope, grad_bias, contract_factor_slope))

def attention_backward(normal_rows, feat_low, weights_low, partition_reverse, back_mixed, token_low, back_num, back_den, divider_projection, partition_projection, prefocus_scale):
    number_branches, slice_count, branch_breadth = token_low.shape
    row_count = back_mixed.shape[1]
    back_heads = back_mixed.reshape(number_branches, branch_breadth, row_count)
    back_num_low = back_num.astype(jnp.bfloat16)
    back_weights = product_f32('hse,hem->hsm', token_low, back_heads) + product_f32('hse,hem->hsm', back_num_low, feat_low) + back_den[:, :, None]
    back_feat = product_f32('hse,hsm->hem', back_num_low, weights_low)
    back_middle, partition_energy_slope, grad_temper = partition_reverse(back_weights)
    back_middle_low = back_middle.reshape(number_branches * branch_breadth, row_count).astype(jnp.bfloat16)
    back_feat_low = back_feat.reshape(number_branches * branch_breadth, row_count).astype(jnp.bfloat16)
    normal_low = normal_rows.astype(jnp.bfloat16)
    mix_mid = matmul_f32(normal_low.T, back_middle_low.T)
    mix_feat = matmul_f32(normal_low.T, back_feat_low.T)
    divider_proj_slope = prefocus_scale[:, None] * mix_mid
    partition_proj_slope = prefocus_scale[:, None] * mix_feat
    grad_gain = lax.optimization_barrier(jnp.sum(divider_projection.astype(jnp.float32) * mix_mid + partition_projection.astype(jnp.float32) * mix_feat, axis=1))
    return (divider_proj_slope, partition_proj_slope, grad_temper.reshape(-1), partition_energy_slope, grad_gain)

def reference(mesh_signals, loss_sensitivity, divider_projection, partition_projection, sharpness_axis, partition_energies, asking_projection, lookup_projection, content_projection, prefocus_scale, emit_projection, premlp_scale, expand_factor, expand_offset, contract_factor):
    blocks = mesh_signals.reshape(N_PTS, PTS_DEV, EMBED_SIZE)
    cot_blocks = loss_sensitivity.reshape(N_PTS, PTS_DEV, EMBED_SIZE)

    def front_of(entering_samples):
        return focus_evaluate(entering_samples, prefocus_scale, divider_projection, partition_projection, sharpness_axis, partition_energies)

    def sum_step(carry, entering_samples):
        parts = front_of(entering_samples)
        return ((carry[0] + parts[4], carry[1] + parts[5]), None)
    start_sums = (jnp.zeros((HEADS, SLICES, HEAD_DIM), jnp.float32), jnp.zeros((HEADS, SLICES), jnp.float32))
    (total_num, total_den), unused = lax.scan(sum_step, start_sums, blocks)
    token_out, token_back = jax.vjp(token_attention, total_num, total_den, asking_projection, lookup_projection, content_projection)
    token_low = token_out.astype(jnp.bfloat16)

    def mix_step(carry, pair):
        entering_samples, cot_rows = pair
        parts = front_of(entering_samples)
        mixed = deslice_heads(parts[2], token_low)
        block_result, back_mixed, grads = mixer_pass(mixed, entering_samples, cot_rows, emit_projection, premlp_scale, expand_factor, expand_offset, contract_factor)
        terms = grads + (token_gradient(parts[2], back_mixed),)
        return (jax.tree.map(jnp.add, carry, terms), (block_result, back_mixed))
    start_mix = (jnp.zeros((EMBED_SIZE, EMBED_SIZE), jnp.float32), jnp.zeros((EMBED_SIZE,), jnp.float32), jnp.zeros((EMBED_SIZE, FF), jnp.float32), jnp.zeros((FF,), jnp.float32), jnp.zeros((FF, EMBED_SIZE), jnp.float32), jnp.zeros((HEADS, SLICES, HEAD_DIM), jnp.float32))
    mix_sums, (outputs, back_all) = lax.scan(mix_step, start_mix, (blocks, cot_blocks))
    emit_proj_slope, premlp_scale_slope, expand_factor_slope, expand_offset_slope, contract_factor_slope, token_grad = mix_sums
    back_num, back_den, asking_proj_slope, lookup_proj_slope, content_proj_slope = token_back(token_grad)

    def back_step(carry, pair):
        entering_samples, back_mixed = pair
        parts = front_of(entering_samples)
        terms = attention_backward(parts[0], parts[1], parts[2], parts[3], back_mixed, token_low, back_num, back_den, divider_projection, partition_projection, prefocus_scale)
        return (jax.tree.map(jnp.add, carry, terms), None)
    start_back = (jnp.zeros((EMBED_SIZE, EMBED_SIZE), jnp.float32), jnp.zeros((EMBED_SIZE, EMBED_SIZE), jnp.float32), jnp.zeros((EMBED_SIZE,), jnp.float32), jnp.zeros((HEADS, HEAD_DIM, SLICES), jnp.float32), jnp.zeros((EMBED_SIZE,), jnp.float32))
    reverse_totals, unused_back = lax.scan(back_step, start_back, (blocks, back_all))
    divider_proj_slope, partition_proj_slope, sharpness_axis_slope, partition_energy_slope, prefocus_scale_slope = reverse_totals
    block_result = outputs.reshape(POINTS, EMBED_SIZE)
    return (block_result, divider_proj_slope, partition_proj_slope, sharpness_axis_slope, partition_energy_slope, asking_proj_slope, lookup_proj_slope, content_proj_slope, prefocus_scale_slope, emit_proj_slope, premlp_scale_slope, expand_factor_slope, expand_offset_slope, contract_factor_slope)
```

```python
import functools

import jax
import jax.numpy as jnp
from jax import lax
from jax.experimental import pallas as pl
from jax.experimental.pallas import tpu as pltpu
from jax.sharding import PartitionSpec as P

SCORE_LIMIT = 30.0
NORM_EPS = 1e-05
GELU_SCALE = 0.7978845608028654
GELU_CUBE = 0.044715
HIGHEST = lax.Precision.HIGHEST
PAD = 16


NN = (((1,), (0,)), ((), ()))
NT = (((1,), (1,)), ((), ()))
TN = (((0,), (0,)), ((), ()))


def dot(a, b, numbers=NN, precision=None):
    return lax.dot_general(a, b, numbers, precision=precision, preferred_element_type=jnp.float32)


def axis_groups(axis):
    size = lax.axis_size(axis)
    groups = []
    stride = 1
    step = 2 if axis == "pts" else 4
    while stride < size:
        count = min(step, size // stride)
        groups.append((axis, stride, count))
        stride *= count
        step = 4
    return groups


def swap(value, axis, distance):
    size = lax.axis_size(axis)
    return lax.ppermute(value, axis, [(i, i ^ distance) for i in range(size)])


def tree_sum(parts):
    while len(parts) > 1:
        parts = [parts[i] + parts[i + 1] for i in range(0, len(parts), 2)]
    return parts[0]


def group_sum(value, group):
    axis, stride, count = group
    return tree_sum([value] + [swap(value, axis, m * stride) for m in range(1, count)])


def position(group):
    axis, stride, count = group
    return (lax.axis_index(axis) // stride) % count


def group_scatter(value, group):
    axis, stride, count = group
    block = value.shape[0] // count
    me = position(group)
    parts = []
    for m in range(count):
        piece = lax.dynamic_slice_in_dim(value, (me ^ m) * block, block, 0)
        parts.append(swap(piece, axis, m * stride) if m else piece)
    return tree_sum(parts)


def group_gather(value, group):
    axis, stride, count = group
    block = value.shape[0]
    me = position(group)
    result = jnp.zeros((count * block,) + value.shape[1:], value.dtype)
    for m in range(count):
        piece = swap(value, axis, m * stride) if m else value
        result = lax.dynamic_update_slice_in_dim(result, piece, (me ^ m) * block, 0)
    return result


def all_sum(value, groups):
    for group in groups:
        value = group_sum(value, group)
    return value


def big_sum(value, groups):
    for group in groups:
        value = group_scatter(value, group)
    for group in groups[::-1]:
        value = group_gather(value, group)
    return value


def gather_head(value):
    for group in axis_groups("head"):
        value = group_gather(value, group)
    return value


def same_head(shape, row_span, column_span):
    rows = lax.broadcasted_iota(jnp.int32, shape, 0) // row_span
    columns = lax.broadcasted_iota(jnp.int32, shape, 1) // column_span
    return rows == columns


def fold_heads(full, heads, width, slices):
    kept = jnp.where(same_head(full.shape, width, slices), full, 0.0)
    return jnp.sum(kept.reshape(heads, width, heads * slices), axis=0)


def sharp_terms(raw):
    sharpness = 0.5 + jnp.maximum(raw, 0.0) + jnp.log1p(jnp.exp(-jnp.abs(raw)))
    return 1.0 / sharpness


def front_kernel(
    member_ref,
    x_ref,
    gain_ref,
    high_ref,
    low_ref,
    feat_ref,
    s_ref,
    w_ref,
    m_ref,
    tot_ref,
    z_scr,
    r_scr,
    den_scr,
    *,
    heads,
    slices,
    chunk,
):
    step = pl.program_id(0)
    lanes = heads * slices

    @pl.when(step == 0)
    def _():
        m_ref[...] = jnp.zeros_like(m_ref)
        den_scr[...] = jnp.zeros_like(den_scr)

    x = x_ref[...].astype(jnp.float32)
    centered = x - jnp.mean(x, axis=1, keepdims=True)
    spread = jnp.mean(centered * centered, axis=1, keepdims=True)
    scaled = (centered * lax.rsqrt(spread + NORM_EPS) * gain_ref[...]).astype(jnp.bfloat16)
    s_ref[...] = scaled
    z_scr[...] = dot(high_ref[...], scaled, NT) + dot(low_ref[...], scaled, NT)
    r_scr[...] = sharp_terms(z_scr[lanes : lanes + heads, :]) * (1.0 / SCORE_LIMIT)
    rows = x_ref.shape[0]
    for h in range(heads):
        span = slice(h * slices, (h + 1) * slices)
        for c in range(rows // chunk):
            cols = slice(c * chunk, (c + 1) * chunk)
            z = z_scr[span, cols] * r_scr[h : h + 1, cols]
            raised = jnp.exp(SCORE_LIMIT * jnp.tanh(z))
            weights = raised * (1.0 / jnp.sum(raised, axis=0, keepdims=True))
            w_ref[span, cols] = weights.astype(jnp.bfloat16)
            part = weights[:, 0:128]
            for k in range(1, chunk // 128):
                part = part + weights[:, k * 128 : (k + 1) * 128]
            den_scr[span, :] += part
    m_ref[...] += dot(w_ref[...], scaled)

    @pl.when(step == pl.num_programs(0) - 1)
    def _():
        full = dot(feat_ref[...].astype(jnp.float32), m_ref[...], NT, HIGHEST)
        width = full.shape[0] // heads
        tot_ref[0:width, :] = fold_heads(full, heads, width, slices)
        ones = jnp.ones((8, 128), jnp.float32)
        tot_ref[width : width + 8, :] = dot(ones, den_scr[...], NT, HIGHEST)


def mixer_kernel(
    member_ref,
    x_ref,
    w_ref,
    loss_ref,
    te_ref,
    gain_ref,
    expand_ref,
    expand_t_ref,
    offset_ref,
    contract_ref,
    contract_t_ref,
    token_ref,
    emit_ref,
    block_ref,
    back_ref,
    grads_ref,
    gains_ref,
    tg_ref,
    wr_scr,
    gain_scr,
    *,
    heads,
    slices,
):
    step = pl.program_id(0)
    width = emit_ref.shape[0]

    @pl.when(step == 0)
    def _():
        grads_ref[...] = jnp.zeros_like(grads_ref)
        gain_scr[...] = jnp.zeros_like(gain_scr)
        wr_scr[...] = jnp.zeros_like(wr_scr)

    weights = w_ref[...]
    loss = loss_ref[...]
    residual = x_ref[...].astype(jnp.float32) + dot(weights, te_ref[...], TN)
    centered = residual - jnp.mean(residual, axis=1, keepdims=True)
    spread = jnp.mean(centered * centered, axis=1, keepdims=True)
    rstd = lax.rsqrt(spread + NORM_EPS)
    normal = centered * rstd
    gain = gain_ref[...]
    normed = (normal * gain).astype(jnp.bfloat16)
    inner = dot(normed, expand_ref[...]) + offset_ref[...]
    square = inner * inner
    bent = jnp.tanh(GELU_SCALE * inner * (1.0 + GELU_CUBE * square))
    half = 0.5 * (1.0 + bent)
    active = (inner * half).astype(jnp.bfloat16)
    slope = half + 0.5 * inner * (1.0 - bent * bent) * (
        GELU_SCALE + (3.0 * GELU_CUBE * GELU_SCALE) * square
    )
    block_ref[...] = (residual + dot(active, contract_ref[...])).astype(jnp.bfloat16)
    back_inner = dot(loss, contract_t_ref[...]) * slope
    back_low = back_inner.astype(jnp.bfloat16)
    back_normed = dot(back_low, expand_t_ref[...])
    gained = back_normed * normal
    pulled = back_normed * gain
    mean_pull = jnp.mean(pulled, axis=1, keepdims=True)
    mean_gain = jnp.mean(pulled * normal, axis=1, keepdims=True)
    back_resid = loss.astype(jnp.float32) + rstd * (pulled - mean_pull - normal * mean_gain)
    back = back_resid.astype(jnp.bfloat16)
    back_ref[...] = back
    grads_ref[width : 2 * width, :] += dot(normed, back_low, TN)
    grads_ref[2 * width : 3 * width, :] += dot(active, loss, TN)
    rows = x_ref.shape[0]
    gain_scr[0:8, :] += jnp.sum(gained.reshape(rows // 8, 8, width), axis=0)
    gain_scr[8:16, :] += jnp.sum(back_inner.reshape(rows // 8, 8, width), axis=0)
    wr_scr[...] += dot(weights, back)

    @pl.when(step == pl.num_programs(0) - 1)
    def _():
        grads_ref[0:width, :] = dot(
            token_ref[...].astype(jnp.float32), wr_scr[...], NN, HIGHEST
        )
        full = dot(emit_ref[...].astype(jnp.float32), wr_scr[...], NT, HIGHEST)
        tg_ref[...] = fold_heads(full, heads, full.shape[0] // heads, slices)
        gains_ref[...] = jnp.zeros_like(gains_ref)
        gains_ref[1:2, :] = jnp.sum(gain_scr[0:8, :], axis=0, keepdims=True)
        gains_ref[2:3, :] = jnp.sum(gain_scr[8:16, :], axis=0, keepdims=True)


def back_kernel(
    s_ref,
    back_ref,
    high_ref,
    low_ref,
    te_ref,
    fb_ref,
    den_ref,
    m_ref,
    energy_ref,
    num_ref,
    div_ref,
    part_ref,
    scale_ref,
    gains_ref,
    out_ref,
    z_scr,
    b_scr,
    r_scr,
    d_scr,
    g_scr,
    *,
    heads,
    slices,
    chunk,
    local,
    block,
):
    step = pl.program_id(0)
    lanes = heads * slices

    @pl.when(step == 0)
    def _():
        g_scr[...] = jnp.zeros_like(g_scr)
        d_scr[...] = jnp.zeros_like(d_scr)

    scaled = s_ref[...]
    z_scr[...] = dot(high_ref[...], scaled, NT) + dot(low_ref[...], scaled, NT)
    b_scr[...] = dot(te_ref[...], back_ref[...], NT) + dot(fb_ref[...], scaled, NT)
    raw = z_scr[lanes : lanes + heads, :]
    r_scr[...] = sharp_terms(raw)
    rows = s_ref.shape[0]
    for h in range(heads):
        span = slice(h * slices, (h + 1) * slices)
        for c in range(rows // chunk):
            cols = slice(c * chunk, (c + 1) * chunk)
            inverse = r_scr[h : h + 1, cols]
            z = z_scr[span, cols] * (inverse * (1.0 / SCORE_LIMIT))
            bent = jnp.tanh(z)
            raised = jnp.exp(SCORE_LIMIT * bent)
            weights = raised * (1.0 / jnp.sum(raised, axis=0, keepdims=True))
            back_w = b_scr[span, cols] + jnp.concatenate([den_ref[span, :]] * (chunk // 128), axis=1)
            middle = jnp.sum(weights * back_w, axis=0, keepdims=True)
            q = weights * (back_w - middle) * (1.0 - bent * bent)
            d_scr[span, cols] = (q * inverse).astype(jnp.bfloat16)
            z_scr[lanes + 8 + h : lanes + 9 + h, cols] = jnp.sum(q * z, axis=0, keepdims=True)
    pulled = z_scr[lanes + 8 : lanes + 8 + heads, :] * (-SCORE_LIMIT) * r_scr[...]
    pulled = pulled * (1.0 / (1.0 + jnp.exp(-raw)))
    pulled = jnp.concatenate([pulled, jnp.zeros((PAD - heads, rows), jnp.float32)], axis=0)
    d_scr[lanes : lanes + PAD, :] = pulled.astype(jnp.bfloat16)
    g_scr[...] += dot(d_scr[...], scaled)

    @pl.when(step == pl.num_programs(0) - 1)
    def _():
        grads = g_scr[...]
        div = div_ref[...].astype(jnp.float32)
        part = part_ref[...].astype(jnp.float32)
        div_slope = dot(energy_ref[...], grads, NN, HIGHEST)
        part_slope = dot(num_ref[...].astype(jnp.float32), m_ref[...], NN, HIGHEST)
        mixed = jnp.sum(div * div_slope + part * part_slope, axis=0, keepdims=True)
        mixed = mixed / scale_ref[...]
        full = dot(div, grads, NT, HIGHEST)
        width = full.shape[0] // heads
        energy = fold_heads(full[:, :lanes], heads, width, slices)
        tail = full[:, lanes : lanes + PAD]
        sharp = jnp.where(same_head(tail.shape, width, 1), tail, 0.0)
        sharp = jnp.sum(sharp, axis=1, keepdims=True)
        unit = 2 * width + 16
        for h in range(heads):
            base = (h // local) * block + (h % local) * unit
            own = slice(h * width, (h + 1) * width)
            out_ref[base : base + width, :] = div_slope[own]
            out_ref[base + width : base + 2 * width, :] = part_slope[own]
            pair = jnp.concatenate(
                [
                    energy[:, h * slices : (h + 1) * slices],
                    jnp.broadcast_to(sharp[own], (width, 128 - slices)),
                ],
                axis=1,
            )
            out_ref[base + 2 * width : base + unit, :] = jnp.concatenate(
                [pair[:16], pair[16:]], axis=1
            )
        for g in range(heads // local):
            base = g * block + local * unit
            out_ref[base : base + 8, :] = gains_ref[...]
            out_ref[base : base + 1, :] = mixed
            if base + 8 < (g + 1) * block:
                out_ref[base + 8 : (g + 1) * block, :] = jnp.zeros(
                    (block - local * unit - 8, mixed.shape[1]), jnp.float32
                )


def whole(shape):
    return pl.BlockSpec(shape, lambda i, *refs: (0,) * len(shape))


def params():
    return pltpu.CompilerParams(
        dimension_semantics=("arbitrary",), vmem_limit_bytes=56 * 1024 * 1024
    )


def token_attention(total_num, total_den, asking_projection, lookup_projection, content_projection):
    tokens = total_num / (total_den[:, :, None] + NORM_EPS)
    query_rows = jnp.einsum("hse,hef->hsf", tokens, asking_projection, precision=HIGHEST)
    key_rows = jnp.einsum("hse,hef->hsf", tokens, lookup_projection, precision=HIGHEST)
    value_rows = jnp.einsum("hse,hef->hsf", tokens, content_projection, precision=HIGHEST)
    scores = (
        jnp.einsum("hsf,htf->hst", query_rows, key_rows, precision=HIGHEST)
        * query_rows.shape[-1] ** (-0.5)
    )
    bounded_energies = SCORE_LIMIT * jnp.tanh(scores / SCORE_LIMIT)
    raised = jnp.exp(bounded_energies)
    attend = raised / jnp.sum(raised, axis=-1, keepdims=True)
    return jnp.einsum("hst,htf->hsf", attend, value_rows, precision=HIGHEST)


def block_diagonal(value):
    heads, rows, columns = value.shape
    eye = jnp.eye(heads, dtype=value.dtype)
    return (value[:, :, None, :] * eye[:, None, :, None]).reshape(heads * rows, heads * columns)


def body(
    mesh_signals,
    loss_sensitivity,
    divider_projection,
    partition_projection,
    sharpness_axis,
    partition_energies,
    asking_projection,
    lookup_projection,
    content_projection,
    prefocus_scale,
    emit_projection,
    premlp_scale,
    expand_factor,
    expand_offset,
    contract_factor,
):
    groups = lax.axis_size("head")
    member = lax.axis_index("head")
    rows = loss_sensitivity.shape[0]
    width = mesh_signals.shape[1]
    local, channels, slices = partition_energies.shape
    heads = local * groups
    lanes = heads * slices
    head_groups = axis_groups("head")
    every_group = axis_groups("pts") + head_groups
    place = member.reshape(1).astype(jnp.int32)

    div_t = gather_head(divider_projection.T)
    part_t = gather_head(partition_projection.T)
    energies = gather_head(partition_energies)
    sharp = gather_head(sharpness_axis.reshape(local, channels))
    asking = gather_head(asking_projection)
    lookup = gather_head(lookup_projection)
    content = gather_head(content_projection)

    energy_rows = jnp.concatenate(
        [
            block_diagonal(energies),
            block_diagonal(sharp[:, :, None]),
            jnp.zeros((heads * channels, PAD - heads), jnp.float32),
        ],
        axis=1,
    )
    logits_of = lax.dot_general(
        energy_rows,
        div_t.astype(jnp.float32),
        TN,
        precision=HIGHEST,
        preferred_element_type=jnp.float32,
    )
    high = lax.reduce_precision(logits_of, 8, 7)
    low = (logits_of - high).astype(jnp.bfloat16)
    high = high.astype(jnp.bfloat16)

    tile = 1024
    steps = rows // tile
    total_rows = lanes + PAD
    row_block = pl.BlockSpec((tile, width), lambda i, *refs: (i, 0))
    own_block = pl.BlockSpec((tile, width), lambda i, place: (place[0] * steps + i, 0))
    column_block = pl.BlockSpec((lanes, tile), lambda i, *refs: (0, i))
    scaled, weights, moment, totals = pl.pallas_call(
        functools.partial(front_kernel, heads=heads, slices=slices, chunk=256),
        grid_spec=pltpu.PrefetchScalarGridSpec(
            num_scalar_prefetch=1,
            grid=(steps,),
            in_specs=[
                own_block,
                whole((1, width)),
                whole((total_rows, width)),
                whole((total_rows, width)),
                whole((heads * channels, width)),
            ],
            out_specs=[
                row_block,
                column_block,
                whole((lanes, width)),
                whole((channels + 8, lanes)),
            ],
            scratch_shapes=[
                pltpu.VMEM((total_rows, tile), jnp.float32),
                pltpu.VMEM((heads, tile), jnp.float32),
                pltpu.VMEM((lanes, 128), jnp.float32),
            ],
        ),
        out_shape=[
            jax.ShapeDtypeStruct((rows, width), jnp.bfloat16),
            jax.ShapeDtypeStruct((lanes, rows), jnp.bfloat16),
            jax.ShapeDtypeStruct((lanes, width), jnp.float32),
            jax.ShapeDtypeStruct((channels + 8, lanes), jnp.float32),
        ],
        compiler_params=params(),
        name="front",
    )(place, mesh_signals, prefocus_scale[None, :], high, low, part_t)

    totals = all_sum(totals, every_group)
    total_num = totals[:channels].reshape(channels, heads, slices).transpose(1, 2, 0)
    total_den = totals[channels].reshape(heads, slices)
    token_out, token_back = jax.vjp(
        token_attention, total_num, total_den, asking, lookup, content
    )
    token_low = token_out.astype(jnp.bfloat16)
    token_rows = block_diagonal(token_low.transpose(0, 2, 1))
    token_emit = lax.dot_general(
        token_rows, emit_projection, TN, preferred_element_type=jnp.float32
    ).astype(jnp.bfloat16)

    block_result, back_low, grads, gains, token_grad = pl.pallas_call(
        functools.partial(mixer_kernel, heads=heads, slices=slices),
        grid_spec=pltpu.PrefetchScalarGridSpec(
            num_scalar_prefetch=1,
            grid=(steps,),
            in_specs=[
                own_block,
                column_block,
                row_block,
                whole((lanes, width)),
                whole((1, width)),
                whole(expand_factor.shape),
                whole(expand_factor.shape[::-1]),
                whole((1, expand_offset.shape[0])),
                whole(contract_factor.shape),
                whole(contract_factor.shape[::-1]),
                whole(token_rows.shape),
                whole(emit_projection.shape),
            ],
            out_specs=[
                row_block,
                row_block,
                whole((3 * width, width)),
                whole((8, width)),
                whole((channels, lanes)),
            ],
            scratch_shapes=[
                pltpu.VMEM((lanes, width), jnp.float32),
                pltpu.VMEM((16, width), jnp.float32),
            ],
        ),
        out_shape=[
            jax.ShapeDtypeStruct((rows, width), jnp.bfloat16),
            jax.ShapeDtypeStruct((rows, width), jnp.bfloat16),
            jax.ShapeDtypeStruct((3 * width, width), jnp.float32),
            jax.ShapeDtypeStruct((8, width), jnp.float32),
            jax.ShapeDtypeStruct((channels, lanes), jnp.float32),
        ],
        compiler_params=params(),
        name="mixer",
    )(
        place,
        mesh_signals,
        weights,
        loss_sensitivity,
        token_emit,
        premlp_scale[None, :],
        expand_factor,
        expand_factor.T,
        expand_offset[None, :],
        contract_factor,
        contract_factor.T,
        token_rows,
        emit_projection,
    )

    token_grad = all_sum(token_grad, every_group)
    token_grad = token_grad.reshape(channels, heads, slices).transpose(1, 2, 0)
    back_num, back_den, asking_slope, lookup_slope, content_slope = token_back(token_grad)
    num_low = block_diagonal(back_num.astype(jnp.bfloat16).transpose(0, 2, 1))
    feat_back = lax.dot_general(
        num_low, part_t, TN, preferred_element_type=jnp.float32
    ).astype(jnp.bfloat16)
    den_rows = jnp.broadcast_to(back_den.reshape(lanes, 1), (lanes, 128))

    grads = big_sum(grads, every_group)

    unit = 2 * channels + 16
    grain = 8 * lax.axis_size("pts")
    block = -(-(local * unit + 8) // grain) * grain
    head_grads = pl.pallas_call(
        functools.partial(back_kernel, heads=heads, slices=slices, chunk=256, local=local, block=block),
        grid=(steps,),
        in_specs=[
            row_block,
            row_block,
            whole((total_rows, width)),
            whole((total_rows, width)),
            whole((lanes, width)),
            whole((lanes, width)),
            whole((lanes, 128)),
            whole((lanes, width)),
            whole((heads * channels, total_rows)),
            whole((heads * channels, lanes)),
            whole((heads * channels, width)),
            whole((heads * channels, width)),
            whole((1, width)),
            whole((8, width)),
        ],
        out_specs=whole((groups * block, width)),
        scratch_shapes=[
            pltpu.VMEM((total_rows, tile), jnp.float32),
            pltpu.VMEM((lanes, tile), jnp.float32),
            pltpu.VMEM((heads, tile), jnp.float32),
            pltpu.VMEM((total_rows, tile), jnp.bfloat16),
            pltpu.VMEM((total_rows, width), jnp.float32),
        ],
        out_shape=jax.ShapeDtypeStruct((groups * block, width), jnp.float32),
        compiler_params=params(),
        name="back",
    )(
        scaled,
        back_low,
        high,
        low,
        token_emit,
        feat_back,
        den_rows,
        moment,
        energy_rows,
        num_low,
        div_t,
        part_t,
        prefocus_scale[None, :],
        gains,
    )

    for group in head_groups[::-1]:
        head_grads = group_scatter(head_grads, group)
    head_grads = big_sum(head_grads, axis_groups("pts"))

    own = head_grads[: local * unit].reshape(local, unit, width)
    divider_slope = own[:, :channels].reshape(local * channels, width).T
    partition_slope = own[:, channels : 2 * channels].reshape(local * channels, width).T
    tail = own[:, 2 * channels :]
    tail = jnp.concatenate([tail[:, :, :128], tail[:, :, 128:]], axis=1)
    energy_slope = tail[:, :, :slices]
    sharp_slope = tail[:, :, slices].reshape(-1)
    gain_slopes = head_grads[local * unit : local * unit + 3]

    def own_heads(value):
        return lax.dynamic_slice_in_dim(value, member * local, local, 0)

    return (
        block_result,
        divider_slope,
        partition_slope,
        sharp_slope,
        energy_slope,
        own_heads(asking_slope),
        own_heads(lookup_slope),
        own_heads(content_slope),
        gain_slopes[0],
        grads[:width],
        gain_slopes[1],
        grads[width : 2 * width],
        gain_slopes[2],
        grads[2 * width : 3 * width],
    )


def solution(mesh):
    in_specs = (
        P("pts", None),
        P(("pts", "head"), None),
        P(None, "head"),
        P(None, "head"),
        P("head"),
        P("head", None, None),
        P("head", None, None),
        P("head", None, None),
        P("head", None, None),
        P(),
        P(),
        P(),
        P(),
        P(),
        P(),
    )
    out_specs = (
        P(("pts", "head"), None),
        P(None, "head"),
        P(None, "head"),
        P("head"),
        P("head", None, None),
        P("head", None, None),
        P("head", None, None),
        P("head", None, None),
        P(),
        P(),
        P(),
        P(),
        P(),
        P(),
    )
    return jax.shard_map(body, mesh=mesh, in_specs=in_specs, out_specs=out_specs, check_vma=False)
```

```python
import functools

import jax
import jax.numpy as jnp
from jax import lax
from jax.experimental import pallas as pl
from jax.experimental.pallas import tpu as pltpu
from jax.sharding import PartitionSpec as P


SCORE_LIMIT = 30.0
NORM_EPS = 1e-05
GELU_SCALE = 0.7978845608028654
GELU_CUBE = 0.044715
HIGHEST = lax.Precision.HIGHEST
PAD = 16


NN = (((1,), (0,)), ((), ()))
NT = (((1,), (1,)), ((), ()))
TN = (((0,), (0,)), ((), ()))


def dot(a, b, numbers=NN, precision=None):
    return lax.dot_general(a, b, numbers, precision=precision, preferred_element_type=jnp.float32)


def axis_groups(axis):
    size = lax.axis_size(axis)
    groups = []
    stride = 1
    step = 2 if axis == "pts" else 4
    while stride < size:
        count = min(step, size // stride)
        groups.append((axis, stride, count))
        stride *= count
        step = 4
    return groups


def swap(value, axis, distance):
    size = lax.axis_size(axis)
    return lax.ppermute(value, axis, [(i, i ^ distance) for i in range(size)])


def tree_sum(parts):
    while len(parts) > 1:
        parts = [parts[i] + parts[i + 1] for i in range(0, len(parts), 2)]
    return parts[0]


def group_sum(value, group):
    axis, stride, count = group
    return tree_sum([value] + [swap(value, axis, m * stride) for m in range(1, count)])


def all_sum(value, groups):
    for group in groups:
        value = group_sum(value, group)
    return value


def exchange_sum(value, axes):
    count = 1
    for axis in axes:
        count *= lax.axis_size(axis)
    block = value.shape[0] // count
    pieces = lax.all_to_all(value.reshape(count, block, value.shape[1]), axes, 0, 0, tiled=True)
    return jnp.sum(pieces.astype(jnp.float32), axis=0)


def gather(value, axes):
    count = 1
    for axis in axes:
        count *= lax.axis_size(axis)
    full = lax.all_to_all(
        jnp.broadcast_to(value[None], (count,) + value.shape), axes, 0, 0, tiled=True
    )
    return full.reshape((count * value.shape[0],) + value.shape[1:])


def same_head(shape, row_span, column_span):
    rows = lax.broadcasted_iota(jnp.int32, shape, 0) // row_span
    columns = lax.broadcasted_iota(jnp.int32, shape, 1) // column_span
    return rows == columns


def fold_heads(full, heads, width, slices):
    kept = jnp.where(same_head(full.shape, width, slices), full, 0.0)
    return jnp.sum(kept.reshape(heads, width, heads * slices), axis=0)


def sharp_terms(raw):
    sharpness = 0.5 + jnp.maximum(raw, 0.0) + jnp.log1p(jnp.exp(-jnp.abs(raw)))
    return 1.0 / sharpness


def spread_column(row):
    count = row.shape[1]
    square = jnp.broadcast_to(row, (count, count))
    return jnp.sum(jnp.where(same_head((count, count), 1, 1), square, 0.0), axis=1, keepdims=True)


def pack_kernel(div_ref, part_ref, sharp_ref, energy_ref, ask_ref, look_ref, content_ref, out_ref):
    local, channels, slices = energy_ref.shape
    copies, _, width = out_ref.shape
    div = div_ref[...].astype(jnp.float32)
    part = part_ref[...].astype(jnp.float32)
    for h in range(local):
        base = 3 * channels * h
        own = slice(h * channels, (h + 1) * channels)
        sharp = spread_column(sharp_ref[0:1, own])
        rest = jnp.concatenate(
            [
                energy_ref[h],
                ask_ref[h],
                look_ref[h],
                content_ref[h],
                jnp.broadcast_to(sharp, (channels, width - slices - 3 * channels)),
            ],
            axis=1,
        )
        for g in range(copies):
            out_ref[g, base : base + channels, :] = div[own]
            out_ref[g, base + channels : base + 2 * channels, :] = part[own]
            out_ref[g, base + 2 * channels : base + 3 * channels, :] = rest


def unpack_kernel(
    all_ref, high_ref, low_ref, energy_ref, div_ref, part_ref, ask_ref, look_ref, content_ref
):
    heads, channels, _ = ask_ref.shape
    lanes = high_ref.shape[0] - PAD
    slices = lanes // heads
    energy_ref[...] = jnp.zeros_like(energy_ref)
    for h in range(heads):
        base = 3 * channels * h
        own = slice(h * channels, (h + 1) * channels)
        div_ref[own, :] = all_ref[base : base + channels, :].astype(jnp.bfloat16)
        part_ref[own, :] = all_ref[base + channels : base + 2 * channels, :].astype(jnp.bfloat16)
        rest = all_ref[base + 2 * channels : base + 3 * channels, :]
        energy_ref[own, h * slices : (h + 1) * slices] = rest[:, :slices]
        ask_ref[h] = rest[:, slices : slices + channels]
        look_ref[h] = rest[:, slices + channels : slices + 2 * channels]
        content_ref[h] = rest[:, slices + 2 * channels : slices + 3 * channels]
        spot = slices + 3 * channels
        energy_ref[own, lanes + h : lanes + h + 1] = rest[:, spot : spot + 1]
    logits_of = dot(energy_ref[...], div_ref[...].astype(jnp.float32), TN, HIGHEST)
    high = logits_of.astype(jnp.bfloat16)
    high_ref[...] = high
    low_ref[...] = (logits_of - high.astype(jnp.float32)).astype(jnp.bfloat16)


def finish_kernel(
    in_ref, div_ref, part_ref, energy_ref, sharp_ref, scale_ref, premlp_ref, offset_ref
):
    local, channels, slices = energy_ref.shape
    unit = 2 * channels + 16
    div = []
    part = []
    for h in range(local):
        base = h * unit
        div.append(in_ref[base : base + channels, :])
        part.append(in_ref[base + channels : base + 2 * channels, :])
        tail = in_ref[base + 2 * channels : base + unit, :]
        tail = jnp.concatenate([tail[:, :128], tail[:, 128:]], axis=0)
        energy_ref[h] = tail[:, :slices]
        square = tail[:, slices : slices + channels]
        kept = jnp.where(same_head((channels, channels), 1, 1), square, 0.0)
        sharp_ref[0:1, h * channels : (h + 1) * channels] = jnp.sum(kept, axis=0, keepdims=True)
    div_ref[...] = jnp.concatenate(div, axis=0)
    part_ref[...] = jnp.concatenate(part, axis=0)
    base = local * unit
    scale_ref[...] = in_ref[base : base + 1, :]
    premlp_ref[...] = in_ref[base + 1 : base + 2, :]
    offset_ref[...] = in_ref[base + 2 : base + 3, :]


def norm_kernel(member_ref, x_ref, gain_ref, s_ref):
    x = x_ref[...].astype(jnp.float32)
    centered = x - jnp.mean(x, axis=1, keepdims=True)
    spread = jnp.mean(centered * centered, axis=1, keepdims=True)
    scaled = centered * lax.rsqrt(spread + NORM_EPS) * gain_ref[...]
    s_ref[...] = scaled.astype(jnp.bfloat16)


def front_kernel(
    s_ref,
    high_ref,
    low_ref,
    feat_ref,
    w_ref,
    m_ref,
    tot_ref,
    z_scr,
    r_scr,
    den_scr,
    *,
    heads,
    slices,
    chunk,
):
    step = pl.program_id(0)
    lanes = heads * slices

    @pl.when(step == 0)
    def _():
        m_ref[...] = jnp.zeros_like(m_ref)
        den_scr[...] = jnp.zeros_like(den_scr)

    scaled = s_ref[...]
    z_scr[...] = dot(high_ref[...], scaled, NT) + dot(low_ref[...], scaled, NT)
    r_scr[...] = sharp_terms(z_scr[lanes : lanes + heads, :]) * (1.0 / SCORE_LIMIT)
    rows = s_ref.shape[0]
    for h in range(heads):
        span = slice(h * slices, (h + 1) * slices)
        for c in range(rows // chunk):
            cols = slice(c * chunk, (c + 1) * chunk)
            z = z_scr[span, cols] * r_scr[h : h + 1, cols]
            raised = jnp.exp(SCORE_LIMIT * jnp.tanh(z))
            weights = raised * (1.0 / jnp.sum(raised, axis=0, keepdims=True))
            w_ref[span, cols] = weights.astype(jnp.bfloat16)
            part = weights[:, 0:128]
            for k in range(1, chunk // 128):
                part = part + weights[:, k * 128 : (k + 1) * 128]
            den_scr[span, :] += part
    m_ref[...] += dot(w_ref[...], scaled)

    @pl.when(step == pl.num_programs(0) - 1)
    def _():
        full = dot(feat_ref[...].astype(jnp.float32), m_ref[...], NT, HIGHEST)
        width = full.shape[0] // heads
        tot_ref[0:width, :] = fold_heads(full, heads, width, slices)
        ones = jnp.ones((8, 128), jnp.float32)
        tot_ref[width : width + 8, :] = dot(ones, den_scr[...], NT, HIGHEST)


def mixer_kernel(
    member_ref,
    x_ref,
    w_ref,
    loss_ref,
    te_ref,
    gain_ref,
    expand_ref,
    expand_t_ref,
    offset_ref,
    contract_ref,
    contract_t_ref,
    token_ref,
    emit_ref,
    block_ref,
    back_ref,
    grads_ref,
    gains_ref,
    tg_ref,
    acc_scr,
    wr_scr,
    gain_scr,
    *,
    heads,
    slices,
):
    step = pl.program_id(0)
    width = emit_ref.shape[0]

    @pl.when(step == 0)
    def _():
        acc_scr[...] = jnp.zeros_like(acc_scr)
        gain_scr[...] = jnp.zeros_like(gain_scr)
        wr_scr[...] = jnp.zeros_like(wr_scr)

    weights = w_ref[...]
    loss = loss_ref[...]
    residual = x_ref[...].astype(jnp.float32) + dot(weights, te_ref[...], TN)
    centered = residual - jnp.mean(residual, axis=1, keepdims=True)
    spread = jnp.mean(centered * centered, axis=1, keepdims=True)
    rstd = lax.rsqrt(spread + NORM_EPS)
    normal = centered * rstd
    gain = gain_ref[...]
    normed = (normal * gain).astype(jnp.bfloat16)
    inner = dot(normed, expand_ref[...]) + offset_ref[...]
    square = inner * inner
    bent = jnp.tanh(GELU_SCALE * inner * (1.0 + GELU_CUBE * square))
    half = 0.5 * (1.0 + bent)
    active = (inner * half).astype(jnp.bfloat16)
    slope = half + 0.5 * inner * (1.0 - bent * bent) * (
        GELU_SCALE + (3.0 * GELU_CUBE * GELU_SCALE) * square
    )
    block_ref[...] = (residual + dot(active, contract_ref[...])).astype(jnp.bfloat16)
    back_inner = dot(loss, contract_t_ref[...]) * slope
    back_low = back_inner.astype(jnp.bfloat16)
    back_normed = dot(back_low, expand_t_ref[...])
    gained = back_normed * normal
    pulled = back_normed * gain
    mean_pull = jnp.mean(pulled, axis=1, keepdims=True)
    mean_gain = jnp.mean(pulled * normal, axis=1, keepdims=True)
    back_resid = loss.astype(jnp.float32) + rstd * (pulled - mean_pull - normal * mean_gain)
    back = back_resid.astype(jnp.bfloat16)
    back_ref[...] = back
    acc_scr[0:width, :] += dot(normed, back_low, TN)
    acc_scr[width : 2 * width, :] += dot(active, loss, TN)
    rows = x_ref.shape[0]
    gain_scr[0:8, :] += jnp.sum(gained.reshape(rows // 8, 8, width), axis=0)
    gain_scr[8:16, :] += jnp.sum(back_inner.reshape(rows // 8, 8, width), axis=0)
    wr_scr[...] += dot(weights, back)

    @pl.when(step == pl.num_programs(0) - 1)
    def _():
        grads_ref[0:width, :] = dot(
            token_ref[...].astype(jnp.float32), wr_scr[...], NN, HIGHEST
        ).astype(jnp.bfloat16)
        grads_ref[width : 3 * width, :] = acc_scr[...].astype(jnp.bfloat16)
        full = dot(emit_ref[...].astype(jnp.float32), wr_scr[...], NT, HIGHEST)
        tg_ref[...] = fold_heads(full, heads, full.shape[0] // heads, slices)
        gains_ref[...] = jnp.zeros_like(gains_ref)
        gains_ref[1:2, :] = jnp.sum(gain_scr[0:8, :], axis=0, keepdims=True)
        gains_ref[2:3, :] = jnp.sum(gain_scr[8:16, :], axis=0, keepdims=True)


def back_kernel(
    s_ref,
    back_ref,
    high_ref,
    low_ref,
    te_ref,
    fb_ref,
    den_ref,
    m_ref,
    energy_ref,
    num_ref,
    div_ref,
    part_ref,
    scale_ref,
    gains_ref,
    out_ref,
    z_scr,
    b_scr,
    r_scr,
    d_scr,
    g_scr,
    *,
    heads,
    slices,
    chunk,
    local,
    block,
):
    step = pl.program_id(0)
    lanes = heads * slices

    @pl.when(step == 0)
    def _():
        g_scr[...] = jnp.zeros_like(g_scr)
        d_scr[...] = jnp.zeros_like(d_scr)

    scaled = s_ref[...]
    z_scr[...] = dot(high_ref[...], scaled, NT) + dot(low_ref[...], scaled, NT)
    b_scr[...] = dot(te_ref[...], back_ref[...], NT) + dot(fb_ref[...], scaled, NT)
    raw = z_scr[lanes : lanes + heads, :]
    r_scr[...] = sharp_terms(raw)
    rows = s_ref.shape[0]
    for h in range(heads):
        span = slice(h * slices, (h + 1) * slices)
        for c in range(rows // chunk):
            cols = slice(c * chunk, (c + 1) * chunk)
            inverse = r_scr[h : h + 1, cols]
            z = z_scr[span, cols] * (inverse * (1.0 / SCORE_LIMIT))
            bent = jnp.tanh(z)
            raised = jnp.exp(SCORE_LIMIT * bent)
            weights = raised * (1.0 / jnp.sum(raised, axis=0, keepdims=True))
            back_w = b_scr[span, cols] + jnp.concatenate([den_ref[span, :]] * (chunk // 128), axis=1)
            middle = jnp.sum(weights * back_w, axis=0, keepdims=True)
            q = weights * (back_w - middle) * (1.0 - bent * bent)
            d_scr[span, cols] = (q * inverse).astype(jnp.bfloat16)
            z_scr[lanes + 8 + h : lanes + 9 + h, cols] = jnp.sum(q * z, axis=0, keepdims=True)
    pulled = z_scr[lanes + 8 : lanes + 8 + heads, :] * (-SCORE_LIMIT) * r_scr[...]
    pulled = pulled * (1.0 / (1.0 + jnp.exp(-raw)))
    pulled = jnp.concatenate([pulled, jnp.zeros((PAD - heads, rows), jnp.float32)], axis=0)
    d_scr[lanes : lanes + PAD, :] = pulled.astype(jnp.bfloat16)
    g_scr[...] += dot(d_scr[...], scaled)

    @pl.when(step == pl.num_programs(0) - 1)
    def _():
        grads = g_scr[...]
        div = div_ref[...].astype(jnp.float32)
        part = part_ref[...].astype(jnp.float32)
        div_slope = dot(energy_ref[...], grads, NN, HIGHEST)
        part_slope = dot(num_ref[...].astype(jnp.float32), m_ref[...], NN, HIGHEST)
        mixed = jnp.sum(div * div_slope + part * part_slope, axis=0, keepdims=True)
        mixed = mixed / scale_ref[...]
        full = dot(div, grads, NT, HIGHEST)
        width = full.shape[0] // heads
        energy = fold_heads(full[:, :lanes], heads, width, slices)
        tail = full[:, lanes : lanes + PAD]
        sharp = jnp.where(same_head(tail.shape, width, 1), tail, 0.0)
        sharp = jnp.sum(sharp, axis=1, keepdims=True)
        unit = 2 * width + 16
        for h in range(heads):
            base = (h // local) * block + (h % local) * unit
            own = slice(h * width, (h + 1) * width)
            out_ref[base : base + width, :] = div_slope[own].astype(jnp.bfloat16)
            out_ref[base + width : base + 2 * width, :] = part_slope[own].astype(
                jnp.bfloat16
            )
            pair = jnp.concatenate(
                [
                    energy[:, h * slices : (h + 1) * slices],
                    jnp.broadcast_to(sharp[own], (width, 128 - slices)),
                ],
                axis=1,
            )
            out_ref[base + 2 * width : base + unit, :] = jnp.concatenate(
                [pair[:16], pair[16:]], axis=1
            ).astype(jnp.bfloat16)
        for g in range(heads // local):
            base = g * block + local * unit
            rows_left = block - local * unit
            tail = gains_ref[...] + jnp.where(
                lax.broadcasted_iota(jnp.int32, gains_ref.shape, 0) == 0, mixed, 0.0
            )
            if rows_left > 8:
                tail = jnp.concatenate(
                    [tail, jnp.zeros((rows_left - 8, mixed.shape[1]), jnp.float32)], axis=0
                )
            out_ref[base : base + rows_left, :] = tail.astype(jnp.bfloat16)


def cost(units, rows, width):
    return pl.CostEstimate(
        flops=2 * units * rows * width * width,
        transcendentals=4 * rows * width,
        bytes_accessed=units * rows * width,
    )


def whole(shape):
    return pl.BlockSpec(shape, lambda i, *refs: (0,) * len(shape))


def params():
    return pltpu.CompilerParams(
        dimension_semantics=("arbitrary",), vmem_limit_bytes=56 * 1024 * 1024
    )


def token_attention(total_num, total_den, asking_projection, lookup_projection, content_projection):
    tokens = total_num / (total_den[:, :, None] + NORM_EPS)
    query_rows = jnp.einsum("hse,hef->hsf", tokens, asking_projection, precision=HIGHEST)
    key_rows = jnp.einsum("hse,hef->hsf", tokens, lookup_projection, precision=HIGHEST)
    value_rows = jnp.einsum("hse,hef->hsf", tokens, content_projection, precision=HIGHEST)
    scores = (
        jnp.einsum("hsf,htf->hst", query_rows, key_rows, precision=HIGHEST)
        * query_rows.shape[-1] ** (-0.5)
    )
    bounded_energies = SCORE_LIMIT * jnp.tanh(scores / SCORE_LIMIT)
    raised = jnp.exp(bounded_energies)
    attend = raised / jnp.sum(raised, axis=-1, keepdims=True)
    return jnp.einsum("hst,htf->hsf", attend, value_rows, precision=HIGHEST)


def block_diagonal(value):
    heads, rows, columns = value.shape
    eye = jnp.eye(heads, dtype=value.dtype)
    return (value[:, :, None, :] * eye[:, None, :, None]).reshape(heads * rows, heads * columns)


def body(
    mesh_signals,
    loss_sensitivity,
    divider_projection,
    partition_projection,
    sharpness_axis,
    partition_energies,
    asking_projection,
    lookup_projection,
    content_projection,
    prefocus_scale,
    emit_projection,
    premlp_scale,
    expand_factor,
    expand_offset,
    contract_factor,
):
    groups = lax.axis_size("head")
    member = lax.axis_index("head")
    rows = loss_sensitivity.shape[0]
    width = mesh_signals.shape[1]
    local, channels, slices = partition_energies.shape
    heads = local * groups
    lanes = heads * slices
    every_group = axis_groups("pts") + axis_groups("head")
    place = member.reshape(1).astype(jnp.int32)

    packed = pl.pallas_call(
        pack_kernel,
        out_shape=jax.ShapeDtypeStruct((groups, 3 * local * channels, width), jnp.float32),
        name="pack",
    )(
        divider_projection.T,
        partition_projection.T,
        sharpness_axis[None, :],
        partition_energies,
        asking_projection,
        lookup_projection,
        content_projection,
    )
    packed = lax.all_to_all(packed, "head", 0, 0, tiled=True)
    packed = packed.reshape(3 * heads * channels, width)
    square = jax.ShapeDtypeStruct((heads, channels, channels), jnp.float32)
    high, low, energy_rows, div_t, part_t, asking, lookup, content = pl.pallas_call(
        unpack_kernel,
        out_shape=[
            jax.ShapeDtypeStruct((lanes + PAD, width), jnp.bfloat16),
            jax.ShapeDtypeStruct((lanes + PAD, width), jnp.bfloat16),
            jax.ShapeDtypeStruct((heads * channels, lanes + PAD), jnp.float32),
            jax.ShapeDtypeStruct((heads * channels, width), jnp.bfloat16),
            jax.ShapeDtypeStruct((heads * channels, width), jnp.bfloat16),
            square,
            square,
            square,
        ],
        name="unpack",
    )(packed)

    tile = 1024
    steps = rows // tile
    total_rows = lanes + PAD
    row_block = pl.BlockSpec((tile, width), lambda i, *refs: (i, 0))
    own_block = pl.BlockSpec((tile, width), lambda i, place: (place[0] * steps + i, 0))
    column_block = pl.BlockSpec((lanes, tile), lambda i, *refs: (0, i))
    scaled = pl.pallas_call(
        norm_kernel,
        grid_spec=pltpu.PrefetchScalarGridSpec(
            num_scalar_prefetch=1,
            grid=(steps,),
            in_specs=[own_block, whole((1, width))],
            out_specs=row_block,
        ),
        out_shape=jax.ShapeDtypeStruct((rows, width), jnp.bfloat16),
        compiler_params=params(),
        cost_estimate=cost(8, rows, width),
        name="norm",
    )(place, mesh_signals, prefocus_scale[None, :])
    weights, moment, totals = pl.pallas_call(
        functools.partial(front_kernel, heads=heads, slices=slices, chunk=256),
        grid=(steps,),
        in_specs=[
            row_block,
            whole((total_rows, width)),
            whole((total_rows, width)),
            whole((heads * channels, width)),
        ],
        out_specs=[
            column_block,
            whole((lanes, width)),
            whole((channels + 8, lanes)),
        ],
        scratch_shapes=[
            pltpu.VMEM((total_rows, tile), jnp.float32),
            pltpu.VMEM((heads, tile), jnp.float32),
            pltpu.VMEM((lanes, 128), jnp.float32),
        ],
        out_shape=[
            jax.ShapeDtypeStruct((lanes, rows), jnp.bfloat16),
            jax.ShapeDtypeStruct((lanes, width), jnp.float32),
            jax.ShapeDtypeStruct((channels + 8, lanes), jnp.float32),
        ],
        compiler_params=params(),
        cost_estimate=cost(16, rows, width),
        name="front",
    )(scaled, high, low, part_t)

    totals = all_sum(totals, every_group)
    total_num = totals[:channels].reshape(channels, heads, slices).transpose(1, 2, 0)
    total_den = totals[channels].reshape(heads, slices)
    token_out, token_back = jax.vjp(
        token_attention, total_num, total_den, asking, lookup, content
    )
    token_low = token_out.astype(jnp.bfloat16)
    token_rows = block_diagonal(token_low.transpose(0, 2, 1))
    token_emit = lax.dot_general(
        token_rows, emit_projection, TN, preferred_element_type=jnp.float32
    ).astype(jnp.bfloat16)

    block_result, back_low, grads, gains, token_grad = pl.pallas_call(
        functools.partial(mixer_kernel, heads=heads, slices=slices),
        grid_spec=pltpu.PrefetchScalarGridSpec(
            num_scalar_prefetch=1,
            grid=(steps,),
            in_specs=[
                own_block,
                column_block,
                row_block,
                whole((lanes, width)),
                whole((1, width)),
                whole(expand_factor.shape),
                whole(expand_factor.shape[::-1]),
                whole((1, expand_offset.shape[0])),
                whole(contract_factor.shape),
                whole(contract_factor.shape[::-1]),
                whole(token_rows.shape),
                whole(emit_projection.shape),
            ],
            out_specs=[
                row_block,
                row_block,
                whole((3 * width, width)),
                whole((8, width)),
                whole((channels, lanes)),
            ],
            scratch_shapes=[
                pltpu.VMEM((2 * width, width), jnp.float32),
                pltpu.VMEM((lanes, width), jnp.float32),
                pltpu.VMEM((16, width), jnp.float32),
            ],
        ),
        out_shape=[
            jax.ShapeDtypeStruct((rows, width), jnp.bfloat16),
            jax.ShapeDtypeStruct((rows, width), jnp.bfloat16),
            jax.ShapeDtypeStruct((3 * width, width), jnp.bfloat16),
            jax.ShapeDtypeStruct((8, width), jnp.float32),
            jax.ShapeDtypeStruct((channels, lanes), jnp.float32),
        ],
        compiler_params=params(),
        cost_estimate=cost(26, rows, width),
        name="mixer",
    )(
        place,
        mesh_signals,
        weights,
        loss_sensitivity,
        token_emit,
        premlp_scale[None, :],
        expand_factor,
        expand_factor.T,
        expand_offset[None, :],
        contract_factor,
        contract_factor.T,
        token_rows,
        emit_projection,
    )

    for group in every_group:
        token_grad = group_sum(token_grad, group)
    token_grad = token_grad.reshape(channels, heads, slices).transpose(1, 2, 0)
    back_num, back_den, asking_slope, lookup_slope, content_slope = token_back(token_grad)
    num_low = block_diagonal(back_num.astype(jnp.bfloat16).transpose(0, 2, 1))
    feat_back = lax.dot_general(
        num_low, part_t, TN, preferred_element_type=jnp.float32
    ).astype(jnp.bfloat16)
    den_rows = jnp.broadcast_to(back_den.reshape(lanes, 1), (lanes, 128))

    everyone = ("head", "pts")
    grads = exchange_sum(grads, everyone)
    grads = gather(grads, everyone)

    unit = 2 * channels + 16
    grain = 8 * lax.axis_size("pts")
    block = -(-(local * unit + 8) // grain) * grain
    back_call = pl.pallas_call(
        functools.partial(back_kernel, heads=heads, slices=slices, chunk=256, local=local, block=block),
        grid=(steps,),
        in_specs=[
            row_block,
            row_block,
            whole((total_rows, width)),
            whole((total_rows, width)),
            whole((lanes, width)),
            whole((lanes, width)),
            whole((lanes, 128)),
            whole((lanes, width)),
            whole((heads * channels, total_rows)),
            whole((heads * channels, lanes)),
            whole((heads * channels, width)),
            whole((heads * channels, width)),
            whole((1, width)),
            whole((8, width)),
        ],
        out_specs=whole((groups * block, width)),
        scratch_shapes=[
            pltpu.VMEM((total_rows, tile), jnp.float32),
            pltpu.VMEM((lanes, tile), jnp.float32),
            pltpu.VMEM((heads, tile), jnp.float32),
            pltpu.VMEM((total_rows, tile), jnp.bfloat16),
            pltpu.VMEM((total_rows, width), jnp.float32),
        ],
        out_shape=jax.ShapeDtypeStruct((groups * block, width), jnp.bfloat16),
        compiler_params=params(),
        cost_estimate=cost(26, rows, width),
        name="back",
    )
    head_grads = back_call(
        scaled,
        back_low,
        high,
        low,
        token_emit,
        feat_back,
        den_rows,
        moment,
        energy_rows,
        num_low,
        div_t,
        part_t,
        prefocus_scale[None, :],
        gains,
    )

    head_grads, grads = lax.optimization_barrier((head_grads, grads))
    head_grads = gather(exchange_sum(head_grads, everyone), ("pts",))
    row = jax.ShapeDtypeStruct((1, width), jnp.float32)
    flat = jax.ShapeDtypeStruct((local * channels, width), jnp.float32)
    divider_slope, partition_slope, energy_slope, sharp_slope, scale_slope, premlp_slope, offset_slope = (
        pl.pallas_call(
            finish_kernel,
            out_shape=[
                flat,
                flat,
                jax.ShapeDtypeStruct((local, channels, slices), jnp.float32),
                jax.ShapeDtypeStruct((1, local * channels), jnp.float32),
                row,
                row,
                row,
            ],
            name="finish",
        )(head_grads)
    )

    def own_heads(value):
        return lax.dynamic_slice_in_dim(value, member * local, local, 0)

    return (
        block_result,
        divider_slope.T,
        partition_slope.T,
        sharp_slope.reshape(-1),
        energy_slope,
        own_heads(asking_slope),
        own_heads(lookup_slope),
        own_heads(content_slope),
        scale_slope.reshape(-1),
        grads[:width],
        premlp_slope.reshape(-1),
        grads[width : 2 * width],
        offset_slope.reshape(-1),
        grads[2 * width : 3 * width],
    )


def solution(mesh):
    in_specs = (
        P("pts", None),
        P(("pts", "head"), None),
        P(None, "head"),
        P(None, "head"),
        P("head"),
        P("head", None, None),
        P("head", None, None),
        P("head", None, None),
        P("head", None, None),
        P(),
        P(),
        P(),
        P(),
        P(),
        P(),
    )
    out_specs = (
        P(("pts", "head"), None),
        P(None, "head"),
        P(None, "head"),
        P("head"),
        P("head", None, None),
        P("head", None, None),
        P("head", None, None),
        P("head", None, None),
        P(),
        P(),
        P(),
        P(),
        P(),
        P(),
    )
    return jax.shard_map(body, mesh=mesh, in_specs=in_specs, out_specs=out_specs, check_vma=False)
```

```python
import functools

import jax
import jax.numpy as jnp
from jax import lax
from jax.experimental import pallas as pl
from jax.experimental.pallas import tpu as pltpu
from jax.sharding import PartitionSpec as P


SCORE_LIMIT = 30.0
NORM_EPS = 1e-05
GELU_SCALE = 0.7978845608028654
GELU_CUBE = 0.044715
HIGHEST = lax.Precision.HIGHEST
PAD = 16


NN = (((1,), (0,)), ((), ()))
NT = (((1,), (1,)), ((), ()))
TN = (((0,), (0,)), ((), ()))


def dot(a, b, numbers=NN, precision=None):
    return lax.dot_general(a, b, numbers, precision=precision, preferred_element_type=jnp.float32)


def halves(value):
    high = value.astype(jnp.bfloat16)
    return high, (value - high.astype(jnp.float32)).astype(jnp.bfloat16)


def dot_split(a, b, numbers=NN):
    return dot(a, b[0], numbers) + dot(a, b[1], numbers)


def axis_groups(axis):
    size = lax.axis_size(axis)
    groups = []
    stride = 1
    step = 2 if axis == "pts" else 4
    while stride < size:
        count = min(step, size // stride)
        groups.append((axis, stride, count))
        stride *= count
        step = 4
    return groups


def swap(value, axis, distance):
    size = lax.axis_size(axis)
    return lax.ppermute(value, axis, [(i, i ^ distance) for i in range(size)])


def tree_sum(parts):
    while len(parts) > 1:
        parts = [parts[i] + parts[i + 1] for i in range(0, len(parts), 2)]
    return parts[0]


def group_sum(value, group):
    axis, stride, count = group
    return tree_sum([value] + [swap(value, axis, m * stride) for m in range(1, count)])


def all_sum(value, groups):
    for group in groups:
        value = group_sum(value, group)
    return value


def exchange_sum(value, axes):
    count = 1
    for axis in axes:
        count *= lax.axis_size(axis)
    block = value.shape[0] // count
    pieces = lax.all_to_all(value.reshape(count, block, value.shape[1]), axes, 0, 0, tiled=True)
    return jnp.sum(pieces.astype(jnp.float32), axis=0)


def gather(value, axes):
    count = 1
    for axis in axes:
        count *= lax.axis_size(axis)
    full = lax.all_to_all(
        jnp.broadcast_to(value[None], (count,) + value.shape), axes, 0, 0, tiled=True
    )
    return full.reshape((count * value.shape[0],) + value.shape[1:])


def same_head(shape, row_span, column_span):
    rows = lax.broadcasted_iota(jnp.int32, shape, 0) // row_span
    columns = lax.broadcasted_iota(jnp.int32, shape, 1) // column_span
    return rows == columns


def fold_heads(full, heads, width, slices):
    kept = jnp.where(same_head(full.shape, width, slices), full, 0.0)
    return jnp.sum(kept.reshape(heads, width, heads * slices), axis=0)


def sharp_terms(raw):
    sharpness = 0.5 + jnp.maximum(raw, 0.0) + jnp.log1p(jnp.exp(-jnp.abs(raw)))
    return 1.0 / sharpness


def spread_column(row):
    count = row.shape[1]
    square = jnp.broadcast_to(row, (count, count))
    return jnp.sum(jnp.where(same_head((count, count), 1, 1), square, 0.0), axis=1, keepdims=True)


def pack_kernel(div_ref, part_ref, sharp_ref, energy_ref, ask_ref, look_ref, content_ref, out_ref):
    local, channels, slices = energy_ref.shape
    copies, _, width = out_ref.shape
    div = div_ref[...].astype(jnp.float32)
    part = part_ref[...].astype(jnp.float32)
    for h in range(local):
        base = 3 * channels * h
        own = slice(h * channels, (h + 1) * channels)
        sharp = spread_column(sharp_ref[0:1, own])
        rest = jnp.concatenate(
            [
                energy_ref[h],
                ask_ref[h],
                look_ref[h],
                content_ref[h],
                jnp.broadcast_to(sharp, (channels, width - slices - 3 * channels)),
            ],
            axis=1,
        )
        for g in range(copies):
            out_ref[g, base : base + channels, :] = div[own]
            out_ref[g, base + channels : base + 2 * channels, :] = part[own]
            out_ref[g, base + 2 * channels : base + 3 * channels, :] = rest


def unpack_kernel(
    all_ref, pair_ref, energy_ref, div_ref, part_ref, ask_ref, look_ref, content_ref
):
    heads, channels, _ = ask_ref.shape
    lanes = pair_ref.shape[0] - PAD
    slices = lanes // heads
    energy_ref[...] = jnp.zeros_like(energy_ref)
    for h in range(heads):
        base = 3 * channels * h
        own = slice(h * channels, (h + 1) * channels)
        div_ref[own, :] = all_ref[base : base + channels, :].astype(jnp.bfloat16)
        part_ref[own, :] = all_ref[base + channels : base + 2 * channels, :].astype(jnp.bfloat16)
        rest = all_ref[base + 2 * channels : base + 3 * channels, :]
        energy_ref[own, h * slices : (h + 1) * slices] = rest[:, :slices]
        ask_ref[h] = rest[:, slices : slices + channels]
        look_ref[h] = rest[:, slices + channels : slices + 2 * channels]
        content_ref[h] = rest[:, slices + 2 * channels : slices + 3 * channels]
        spot = slices + 3 * channels
        energy_ref[own, lanes + h : lanes + h + 1] = rest[:, spot : spot + 1]
    logits_of = dot(energy_ref[...], div_ref[...].astype(jnp.float32), TN, HIGHEST)
    pair_ref[...] = jnp.concatenate(halves(logits_of), axis=1)


def finish_kernel(
    in_ref, div_ref, part_ref, energy_ref, sharp_ref, scale_ref, premlp_ref, offset_ref
):
    local, channels, slices = energy_ref.shape
    unit = 2 * channels + 16
    div = []
    part = []
    for h in range(local):
        base = h * unit
        div.append(in_ref[base : base + channels, :])
        part.append(in_ref[base + channels : base + 2 * channels, :])
        tail = in_ref[base + 2 * channels : base + unit, :]
        tail = jnp.concatenate([tail[:, :128], tail[:, 128:]], axis=0)
        energy_ref[h] = tail[:, :slices]
        square = tail[:, slices : slices + channels]
        kept = jnp.where(same_head((channels, channels), 1, 1), square, 0.0)
        sharp_ref[0:1, h * channels : (h + 1) * channels] = jnp.sum(kept, axis=0, keepdims=True)
    div_ref[...] = jnp.concatenate(div, axis=0)
    part_ref[...] = jnp.concatenate(part, axis=0)
    base = local * unit
    scale_ref[...] = in_ref[base : base + 1, :]
    premlp_ref[...] = in_ref[base + 1 : base + 2, :]
    offset_ref[...] = in_ref[base + 2 : base + 3, :]


def norm_kernel(member_ref, x_ref, gain_ref, s_ref):
    x = x_ref[...].astype(jnp.float32)
    centered = x - jnp.mean(x, axis=1, keepdims=True)
    spread = jnp.mean(centered * centered, axis=1, keepdims=True)
    scaled = centered * lax.rsqrt(spread + NORM_EPS) * gain_ref[...]
    s_ref[...] = scaled.astype(jnp.bfloat16)


def front_kernel(
    s_ref,
    pair_ref,
    feat_ref,
    w_ref,
    m_ref,
    tot_ref,
    z_scr,
    r_scr,
    den_scr,
    *,
    heads,
    slices,
    chunk,
):
    step = pl.program_id(0)
    lanes = heads * slices

    @pl.when(step == 0)
    def _():
        m_ref[...] = jnp.zeros_like(m_ref)
        den_scr[...] = jnp.zeros_like(den_scr)

    scaled = s_ref[...]
    z_scr[...] = dot(pair_ref[...], jnp.concatenate([scaled, scaled], axis=1), NT)
    r_scr[...] = sharp_terms(z_scr[lanes : lanes + heads, :]) * (1.0 / SCORE_LIMIT)
    rows = s_ref.shape[0]
    for h in range(heads):
        span = slice(h * slices, (h + 1) * slices)
        for c in range(rows // chunk):
            cols = slice(c * chunk, (c + 1) * chunk)
            z = z_scr[span, cols] * r_scr[h : h + 1, cols]
            raised = jnp.exp(SCORE_LIMIT * jnp.tanh(z))
            weights = raised * (1.0 / jnp.sum(raised, axis=0, keepdims=True))
            w_ref[span, cols] = weights.astype(jnp.bfloat16)
            part = weights[:, 0:128]
            for k in range(1, chunk // 128):
                part = part + weights[:, k * 128 : (k + 1) * 128]
            den_scr[span, :] += part
    m_ref[...] += dot(w_ref[...], scaled)

    @pl.when(step == pl.num_programs(0) - 1)
    def _():
        full = dot_split(feat_ref[...], halves(m_ref[...]), NT)
        width = full.shape[0] // heads
        tot_ref[0:width, :] = fold_heads(full, heads, width, slices)
        ones = jnp.ones((8, 128), jnp.bfloat16)
        tot_ref[width : width + 8, :] = dot_split(ones, halves(den_scr[...]), NT)


def mixer_kernel(
    member_ref,
    x_ref,
    w_ref,
    loss_ref,
    te_ref,
    gain_ref,
    expand_ref,
    expand_t_ref,
    offset_ref,
    contract_ref,
    contract_t_ref,
    token_ref,
    emit_ref,
    block_ref,
    back_ref,
    grads_ref,
    gains_ref,
    tg_ref,
    acc_scr,
    wr_scr,
    gain_scr,
    *,
    heads,
    slices,
):
    step = pl.program_id(0)
    width = emit_ref.shape[0]

    @pl.when(step == 0)
    def _():
        acc_scr[...] = jnp.zeros_like(acc_scr)
        gain_scr[...] = jnp.zeros_like(gain_scr)
        wr_scr[...] = jnp.zeros_like(wr_scr)

    weights = w_ref[...]
    loss = loss_ref[...]
    residual = x_ref[...].astype(jnp.float32) + dot(weights, te_ref[...], TN)
    centered = residual - jnp.mean(residual, axis=1, keepdims=True)
    spread = jnp.mean(centered * centered, axis=1, keepdims=True)
    rstd = lax.rsqrt(spread + NORM_EPS)
    normal = centered * rstd
    gain = gain_ref[...]
    normed = (normal * gain).astype(jnp.bfloat16)
    inner = dot(normed, expand_ref[...]) + offset_ref[...]
    cubic = (GELU_CUBE * GELU_SCALE) * (inner * inner)
    half = 0.5 * jnp.tanh(inner * (GELU_SCALE + cubic)) + 0.5
    gelu = inner * half
    active = gelu.astype(jnp.bfloat16)
    slope = half + (gelu - gelu * half) * (2.0 * GELU_SCALE + 6.0 * cubic)
    block_ref[...] = (residual + dot(active, contract_ref[...])).astype(jnp.bfloat16)
    back_inner = dot(loss, contract_t_ref[...]) * slope
    back_low = back_inner.astype(jnp.bfloat16)
    back_normed = dot(back_low, expand_t_ref[...])
    pulled = back_normed * gain
    mean_pull = jnp.mean(pulled, axis=1, keepdims=True)
    mean_gain = jnp.mean(pulled * normal, axis=1, keepdims=True)
    back_resid = loss.astype(jnp.float32) + rstd * (pulled - mean_pull - normal * mean_gain)
    back = back_resid.astype(jnp.bfloat16)
    back_ref[...] = back
    acc_scr[0:width, :] += dot(normed, back_low, TN)
    acc_scr[width : 2 * width, :] += dot(active, loss, TN)
    rows = x_ref.shape[0]
    gain_scr[...] += jnp.sum(back_inner.reshape(rows // 8, 8, width), axis=0)
    wr_scr[...] += dot(weights, back)

    @pl.when(step == pl.num_programs(0) - 1)
    def _():
        pieces = halves(wr_scr[...])
        grads_ref[0:width, :] = dot_split(token_ref[...], pieces).astype(jnp.bfloat16)
        grads_ref[width : 3 * width, :] = acc_scr[...].astype(jnp.bfloat16)
        full = dot_split(emit_ref[...], pieces, NT)
        tg_ref[...] = fold_heads(full, heads, full.shape[0] // heads, slices)
        gains_ref[...] = jnp.zeros_like(gains_ref)
        product = halves(expand_ref[...].astype(jnp.float32) * acc_scr[0:width, :])
        total = dot_split(jnp.ones((8, product[0].shape[1]), jnp.bfloat16), product, NT)
        gains_ref[1:2, :] = total[0:1] / gain
        gains_ref[2:3, :] = jnp.sum(gain_scr[...], axis=0, keepdims=True)


def back_kernel(
    s_ref,
    back_ref,
    pair_ref,
    te_ref,
    fb_ref,
    den_ref,
    m_ref,
    energy_ref,
    num_ref,
    div_ref,
    part_ref,
    scale_ref,
    gains_ref,
    out_ref,
    z_scr,
    b_scr,
    r_scr,
    d_scr,
    g_scr,
    *,
    heads,
    slices,
    chunk,
    local,
    block,
):
    step = pl.program_id(0)
    lanes = heads * slices

    @pl.when(step == 0)
    def _():
        g_scr[...] = jnp.zeros_like(g_scr)
        d_scr[...] = jnp.zeros_like(d_scr)

    scaled = s_ref[...]
    z_scr[...] = dot(pair_ref[...], jnp.concatenate([scaled, scaled], axis=1), NT)
    b_scr[...] = dot(
        jnp.concatenate([te_ref[...], fb_ref[...]], axis=1),
        jnp.concatenate([back_ref[...], scaled], axis=1),
        NT,
    )
    raw = z_scr[lanes : lanes + heads, :]
    r_scr[...] = sharp_terms(raw)
    rows = s_ref.shape[0]
    for h in range(heads):
        span = slice(h * slices, (h + 1) * slices)
        for c in range(rows // chunk):
            cols = slice(c * chunk, (c + 1) * chunk)
            inverse = r_scr[h : h + 1, cols]
            z = z_scr[span, cols] * (inverse * (1.0 / SCORE_LIMIT))
            bent = jnp.tanh(z)
            raised = jnp.exp(SCORE_LIMIT * bent)
            weights = raised * (1.0 / jnp.sum(raised, axis=0, keepdims=True))
            back_w = b_scr[span, cols] + jnp.concatenate([den_ref[span, :]] * (chunk // 128), axis=1)
            middle = jnp.sum(weights * back_w, axis=0, keepdims=True)
            q = weights * (back_w - middle) * (1.0 - bent * bent)
            d_scr[span, cols] = (q * inverse).astype(jnp.bfloat16)
            z_scr[lanes + 8 + h : lanes + 9 + h, cols] = jnp.sum(q * z, axis=0, keepdims=True)
    pulled = z_scr[lanes + 8 : lanes + 8 + heads, :] * (-SCORE_LIMIT) * r_scr[...]
    pulled = pulled * (1.0 / (1.0 + jnp.exp(-raw)))
    pulled = jnp.concatenate([pulled, jnp.zeros((PAD - heads, rows), jnp.float32)], axis=0)
    d_scr[lanes : lanes + PAD, :] = pulled.astype(jnp.bfloat16)
    g_scr[...] += dot(d_scr[...], scaled)

    @pl.when(step == pl.num_programs(0) - 1)
    def _():
        grads = g_scr[...]
        div = div_ref[...].astype(jnp.float32)
        part = part_ref[...].astype(jnp.float32)
        pieces = halves(grads)
        energy_high, energy_low = halves(energy_ref[...])
        div_slope = dot_split(energy_high, pieces) + dot(energy_low, pieces[0])
        part_slope = dot_split(num_ref[...], halves(m_ref[...]))
        mixed = jnp.sum(div * div_slope + part * part_slope, axis=0, keepdims=True)
        mixed = mixed / scale_ref[...]
        full = dot_split(div_ref[...], pieces, NT)
        width = full.shape[0] // heads
        energy = fold_heads(full[:, :lanes], heads, width, slices)
        tail = full[:, lanes : lanes + PAD]
        sharp = jnp.where(same_head(tail.shape, width, 1), tail, 0.0)
        sharp = jnp.sum(sharp, axis=1, keepdims=True)
        unit = 2 * width + 16
        for h in range(heads):
            base = (h // local) * block + (h % local) * unit
            own = slice(h * width, (h + 1) * width)
            out_ref[base : base + width, :] = div_slope[own].astype(jnp.bfloat16)
            out_ref[base + width : base + 2 * width, :] = part_slope[own].astype(
                jnp.bfloat16
            )
            pair = jnp.concatenate(
                [
                    energy[:, h * slices : (h + 1) * slices],
                    jnp.broadcast_to(sharp[own], (width, 128 - slices)),
                ],
                axis=1,
            )
            out_ref[base + 2 * width : base + unit, :] = jnp.concatenate(
                [pair[:16], pair[16:]], axis=1
            ).astype(jnp.bfloat16)
        for g in range(heads // local):
            base = g * block + local * unit
            rows_left = block - local * unit
            tail = gains_ref[...] + jnp.where(
                lax.broadcasted_iota(jnp.int32, gains_ref.shape, 0) == 0, mixed, 0.0
            )
            if rows_left > 8:
                tail = jnp.concatenate(
                    [tail, jnp.zeros((rows_left - 8, mixed.shape[1]), jnp.float32)], axis=0
                )
            out_ref[base : base + rows_left, :] = tail.astype(jnp.bfloat16)


def cost(units, rows, width):
    return pl.CostEstimate(
        flops=2 * units * rows * width * width,
        transcendentals=4 * rows * width,
        bytes_accessed=units * rows * width,
    )


def whole(shape):
    return pl.BlockSpec(shape, lambda i, *refs: (0,) * len(shape))


def params():
    return pltpu.CompilerParams(
        dimension_semantics=("arbitrary",), vmem_limit_bytes=56 * 1024 * 1024
    )


def token_attention(total_num, total_den, asking_projection, lookup_projection, content_projection):
    tokens = total_num / (total_den[:, :, None] + NORM_EPS)
    query_rows = jnp.einsum("hse,hef->hsf", tokens, asking_projection, precision=HIGHEST)
    key_rows = jnp.einsum("hse,hef->hsf", tokens, lookup_projection, precision=HIGHEST)
    value_rows = jnp.einsum("hse,hef->hsf", tokens, content_projection, precision=HIGHEST)
    scores = (
        jnp.einsum("hsf,htf->hst", query_rows, key_rows, precision=HIGHEST)
        * query_rows.shape[-1] ** (-0.5)
    )
    bounded_energies = SCORE_LIMIT * jnp.tanh(scores / SCORE_LIMIT)
    raised = jnp.exp(bounded_energies)
    attend = raised / jnp.sum(raised, axis=-1, keepdims=True)
    return jnp.einsum("hst,htf->hsf", attend, value_rows, precision=HIGHEST)


def block_diagonal(value):
    heads, rows, columns = value.shape
    eye = jnp.eye(heads, dtype=value.dtype)
    return (value[:, :, None, :] * eye[:, None, :, None]).reshape(heads * rows, heads * columns)


def body(
    mesh_signals,
    loss_sensitivity,
    divider_projection,
    partition_projection,
    sharpness_axis,
    partition_energies,
    asking_projection,
    lookup_projection,
    content_projection,
    prefocus_scale,
    emit_projection,
    premlp_scale,
    expand_factor,
    expand_offset,
    contract_factor,
):
    groups = lax.axis_size("head")
    member = lax.axis_index("head")
    rows = loss_sensitivity.shape[0]
    width = mesh_signals.shape[1]
    local, channels, slices = partition_energies.shape
    heads = local * groups
    lanes = heads * slices
    every_group = axis_groups("pts") + axis_groups("head")
    place = member.reshape(1).astype(jnp.int32)

    packed = pl.pallas_call(
        pack_kernel,
        out_shape=jax.ShapeDtypeStruct((groups, 3 * local * channels, width), jnp.float32),
        name="pack",
    )(
        divider_projection.T,
        partition_projection.T,
        sharpness_axis[None, :],
        partition_energies,
        asking_projection,
        lookup_projection,
        content_projection,
    )
    packed = lax.all_to_all(packed, "head", 0, 0, tiled=True)
    packed = packed.reshape(3 * heads * channels, width)
    square = jax.ShapeDtypeStruct((heads, channels, channels), jnp.float32)
    pair, energy_rows, div_t, part_t, asking, lookup, content = pl.pallas_call(
        unpack_kernel,
        out_shape=[
            jax.ShapeDtypeStruct((lanes + PAD, 2 * width), jnp.bfloat16),
            jax.ShapeDtypeStruct((heads * channels, lanes + PAD), jnp.float32),
            jax.ShapeDtypeStruct((heads * channels, width), jnp.bfloat16),
            jax.ShapeDtypeStruct((heads * channels, width), jnp.bfloat16),
            square,
            square,
            square,
        ],
        name="unpack",
    )(packed)

    tile = 2048
    steps = rows // tile
    total_rows = lanes + PAD
    row_block = pl.BlockSpec((tile, width), lambda i, *refs: (i, 0))
    own_block = pl.BlockSpec((tile, width), lambda i, place: (place[0] * steps + i, 0))
    column_block = pl.BlockSpec((lanes, tile), lambda i, *refs: (0, i))
    scaled = pl.pallas_call(
        norm_kernel,
        grid_spec=pltpu.PrefetchScalarGridSpec(
            num_scalar_prefetch=1,
            grid=(steps,),
            in_specs=[own_block, whole((1, width))],
            out_specs=row_block,
        ),
        out_shape=jax.ShapeDtypeStruct((rows, width), jnp.bfloat16),
        compiler_params=params(),
        cost_estimate=cost(8, rows, width),
        name="norm",
    )(place, mesh_signals, prefocus_scale[None, :])
    weights, moment, totals = pl.pallas_call(
        functools.partial(front_kernel, heads=heads, slices=slices, chunk=256),
        grid=(steps,),
        in_specs=[
            row_block,
            whole((total_rows, 2 * width)),
            whole((heads * channels, width)),
        ],
        out_specs=[
            column_block,
            whole((lanes, width)),
            whole((channels + 8, lanes)),
        ],
        scratch_shapes=[
            pltpu.VMEM((total_rows, tile), jnp.float32),
            pltpu.VMEM((heads, tile), jnp.float32),
            pltpu.VMEM((lanes, 128), jnp.float32),
        ],
        out_shape=[
            jax.ShapeDtypeStruct((lanes, rows), jnp.bfloat16),
            jax.ShapeDtypeStruct((lanes, width), jnp.float32),
            jax.ShapeDtypeStruct((channels + 8, lanes), jnp.float32),
        ],
        compiler_params=params(),
        cost_estimate=cost(16, rows, width),
        name="front",
    )(scaled, pair, part_t)

    totals = all_sum(totals, every_group)
    total_num = totals[:channels].reshape(channels, heads, slices).transpose(1, 2, 0)
    total_den = totals[channels].reshape(heads, slices)
    token_out, token_back = jax.vjp(
        token_attention, total_num, total_den, asking, lookup, content
    )
    token_low = token_out.astype(jnp.bfloat16)
    token_rows = block_diagonal(token_low.transpose(0, 2, 1))
    token_emit = lax.dot_general(
        token_rows, emit_projection, TN, preferred_element_type=jnp.float32
    ).astype(jnp.bfloat16)

    block_result, back_low, grads, gains, token_grad = pl.pallas_call(
        functools.partial(mixer_kernel, heads=heads, slices=slices),
        grid_spec=pltpu.PrefetchScalarGridSpec(
            num_scalar_prefetch=1,
            grid=(steps,),
            in_specs=[
                own_block,
                column_block,
                row_block,
                whole((lanes, width)),
                whole((1, width)),
                whole(expand_factor.shape),
                whole(expand_factor.shape[::-1]),
                whole((1, expand_offset.shape[0])),
                whole(contract_factor.shape),
                whole(contract_factor.shape[::-1]),
                whole(token_rows.shape),
                whole(emit_projection.shape),
            ],
            out_specs=[
                row_block,
                row_block,
                whole((3 * width, width)),
                whole((8, width)),
                whole((channels, lanes)),
            ],
            scratch_shapes=[
                pltpu.VMEM((2 * width, width), jnp.float32),
                pltpu.VMEM((lanes, width), jnp.float32),
                pltpu.VMEM((8, width), jnp.float32),
            ],
        ),
        out_shape=[
            jax.ShapeDtypeStruct((rows, width), jnp.bfloat16),
            jax.ShapeDtypeStruct((rows, width), jnp.bfloat16),
            jax.ShapeDtypeStruct((3 * width, width), jnp.bfloat16),
            jax.ShapeDtypeStruct((8, width), jnp.float32),
            jax.ShapeDtypeStruct((channels, lanes), jnp.float32),
        ],
        compiler_params=params(),
        cost_estimate=cost(26, rows, width),
        name="mixer",
    )(
        place,
        mesh_signals,
        weights,
        loss_sensitivity,
        token_emit,
        premlp_scale[None, :],
        expand_factor,
        expand_factor.T,
        expand_offset[None, :],
        contract_factor,
        contract_factor.T,
        token_rows,
        emit_projection,
    )

    for group in every_group:
        token_grad = group_sum(token_grad, group)
    token_grad = token_grad.reshape(channels, heads, slices).transpose(1, 2, 0)
    back_num, back_den, asking_slope, lookup_slope, content_slope = token_back(token_grad)
    num_low = block_diagonal(back_num.astype(jnp.bfloat16).transpose(0, 2, 1))
    feat_back = lax.dot_general(
        num_low, part_t, TN, preferred_element_type=jnp.float32
    ).astype(jnp.bfloat16)
    den_rows = jnp.broadcast_to(back_den.reshape(lanes, 1), (lanes, 128))

    everyone = ("head", "pts")
    grads = exchange_sum(grads, everyone)
    grads = gather(grads, everyone)

    unit = 2 * channels + 16
    grain = 8 * lax.axis_size("pts")
    block = -(-(local * unit + 8) // grain) * grain
    back_call = pl.pallas_call(
        functools.partial(back_kernel, heads=heads, slices=slices, chunk=256, local=local, block=block),
        grid=(steps,),
        in_specs=[
            row_block,
            row_block,
            whole((total_rows, 2 * width)),
            whole((lanes, width)),
            whole((lanes, width)),
            whole((lanes, 128)),
            whole((lanes, width)),
            whole((heads * channels, total_rows)),
            whole((heads * channels, lanes)),
            whole((heads * channels, width)),
            whole((heads * channels, width)),
            whole((1, width)),
            whole((8, width)),
        ],
        out_specs=whole((groups * block, width)),
        scratch_shapes=[
            pltpu.VMEM((total_rows, tile), jnp.float32),
            pltpu.VMEM((lanes, tile), jnp.float32),
            pltpu.VMEM((heads, tile), jnp.float32),
            pltpu.VMEM((total_rows, tile), jnp.bfloat16),
            pltpu.VMEM((total_rows, width), jnp.float32),
        ],
        out_shape=jax.ShapeDtypeStruct((groups * block, width), jnp.bfloat16),
        compiler_params=params(),
        cost_estimate=cost(26, rows, width),
        name="back",
    )
    head_grads = back_call(
        scaled,
        back_low,
        pair,
        token_emit,
        feat_back,
        den_rows,
        moment,
        energy_rows,
        num_low,
        div_t,
        part_t,
        prefocus_scale[None, :],
        gains,
    )

    head_grads, grads = lax.optimization_barrier((head_grads, grads))
    head_grads = gather(exchange_sum(head_grads, everyone), ("pts",))
    row = jax.ShapeDtypeStruct((1, width), jnp.float32)
    flat = jax.ShapeDtypeStruct((local * channels, width), jnp.float32)
    divider_slope, partition_slope, energy_slope, sharp_slope, scale_slope, premlp_slope, offset_slope = (
        pl.pallas_call(
            finish_kernel,
            out_shape=[
                flat,
                flat,
                jax.ShapeDtypeStruct((local, channels, slices), jnp.float32),
                jax.ShapeDtypeStruct((1, local * channels), jnp.float32),
                row,
                row,
                row,
            ],
            name="finish",
        )(head_grads)
    )

    def own_heads(value):
        return lax.dynamic_slice_in_dim(value, member * local, local, 0)

    return (
        block_result,
        divider_slope.T,
        partition_slope.T,
        sharp_slope.reshape(-1),
        energy_slope,
        own_heads(asking_slope),
        own_heads(lookup_slope),
        own_heads(content_slope),
        scale_slope.reshape(-1),
        grads[:width],
        premlp_slope.reshape(-1),
        grads[width : 2 * width],
        offset_slope.reshape(-1),
        grads[2 * width : 3 * width],
    )


def solution(mesh):
    in_specs = (
        P("pts", None),
        P(("pts", "head"), None),
        P(None, "head"),
        P(None, "head"),
        P("head"),
        P("head", None, None),
        P("head", None, None),
        P("head", None, None),
        P("head", None, None),
        P(),
        P(),
        P(),
        P(),
        P(),
        P(),
    )
    out_specs = (
        P(("pts", "head"), None),
        P(None, "head"),
        P(None, "head"),
        P("head"),
        P("head", None, None),
        P("head", None, None),
        P("head", None, None),
        P("head", None, None),
        P(),
        P(),
        P(),
        P(),
        P(),
        P(),
    )
    return jax.shard_map(body, mesh=mesh, in_specs=in_specs, out_specs=out_specs, check_vma=False)
```

```python
import functools

import jax
import jax.numpy as jnp
from jax import lax
from jax.experimental import pallas as pl
from jax.experimental.pallas import tpu as pltpu
from jax.sharding import PartitionSpec as P


SCORE_LIMIT = 30.0
NORM_EPS = 1e-05
GELU_SCALE = 0.7978845608028654
GELU_CUBE = 0.044715
HIGHEST = lax.Precision.HIGHEST
PAD = 16


NN = (((1,), (0,)), ((), ()))
NT = (((1,), (1,)), ((), ()))
TN = (((0,), (0,)), ((), ()))


def dot(a, b, numbers=NN, precision=None):
    return lax.dot_general(a, b, numbers, precision=precision, preferred_element_type=jnp.float32)


def halves(value):
    high = value.astype(jnp.bfloat16)
    return high, (value - high.astype(jnp.float32)).astype(jnp.bfloat16)


def dot_split(a, b, numbers=NN):
    return dot(a, b[0], numbers) + dot(a, b[1], numbers)


def axis_groups(axis):
    size = lax.axis_size(axis)
    groups = []
    stride = 1
    step = 2 if axis == "pts" else 4
    while stride < size:
        count = min(step, size // stride)
        groups.append((axis, stride, count))
        stride *= count
        step = 4
    return groups


def swap(value, axis, distance):
    size = lax.axis_size(axis)
    return lax.ppermute(value, axis, [(i, i ^ distance) for i in range(size)])


def tree_sum(parts):
    while len(parts) > 1:
        parts = [parts[i] + parts[i + 1] for i in range(0, len(parts), 2)]
    return parts[0]


def group_sum(value, group):
    axis, stride, count = group
    return tree_sum([value] + [swap(value, axis, m * stride) for m in range(1, count)])


def all_sum(value, groups):
    for group in groups:
        value = group_sum(value, group)
    return value


def exchange_sum(value, axes):
    count = 1
    for axis in axes:
        count *= lax.axis_size(axis)
    block = value.shape[0] // count
    pieces = lax.all_to_all(value.reshape(count, block, value.shape[1]), axes, 0, 0, tiled=True)
    return jnp.sum(pieces.astype(jnp.float32), axis=0)


def gather(value, axes):
    count = 1
    for axis in axes:
        count *= lax.axis_size(axis)
    full = lax.all_to_all(
        jnp.broadcast_to(value[None], (count,) + value.shape), axes, 0, 0, tiled=True
    )
    return full.reshape((count * value.shape[0],) + value.shape[1:])


def same_head(shape, row_span, column_span):
    rows = lax.broadcasted_iota(jnp.int32, shape, 0) // row_span
    columns = lax.broadcasted_iota(jnp.int32, shape, 1) // column_span
    return rows == columns


def fold_heads(full, heads, width, slices):
    kept = jnp.where(same_head(full.shape, width, slices), full, 0.0)
    return jnp.sum(kept.reshape(heads, width, heads * slices), axis=0)


def sharp_terms(raw):
    sharpness = 0.5 + jnp.maximum(raw, 0.0) + jnp.log1p(jnp.exp(-jnp.abs(raw)))
    return 1.0 / sharpness


def spread_column(row):
    count = row.shape[1]
    square = jnp.broadcast_to(row, (count, count))
    return jnp.sum(jnp.where(same_head((count, count), 1, 1), square, 0.0), axis=1, keepdims=True)


def pack_kernel(div_ref, part_ref, sharp_ref, energy_ref, ask_ref, look_ref, content_ref, out_ref):
    local, channels, slices = energy_ref.shape
    copies, _, width = out_ref.shape
    div = div_ref[...].astype(jnp.float32)
    part = part_ref[...].astype(jnp.float32)
    for h in range(local):
        base = 3 * channels * h
        own = slice(h * channels, (h + 1) * channels)
        sharp = spread_column(sharp_ref[0:1, own])
        rest = jnp.concatenate(
            [
                energy_ref[h],
                ask_ref[h],
                look_ref[h],
                content_ref[h],
                jnp.broadcast_to(sharp, (channels, width - slices - 3 * channels)),
            ],
            axis=1,
        )
        for g in range(copies):
            out_ref[g, base : base + channels, :] = div[own]
            out_ref[g, base + channels : base + 2 * channels, :] = part[own]
            out_ref[g, base + 2 * channels : base + 3 * channels, :] = rest


def unpack_kernel(
    all_ref, pair_ref, energy_ref, div_ref, part_ref, ask_ref, look_ref, content_ref
):
    heads, channels, _ = ask_ref.shape
    lanes = pair_ref.shape[0] - PAD
    slices = lanes // heads
    energy_ref[...] = jnp.zeros_like(energy_ref)
    for h in range(heads):
        base = 3 * channels * h
        own = slice(h * channels, (h + 1) * channels)
        div_ref[own, :] = all_ref[base : base + channels, :].astype(jnp.bfloat16)
        part_ref[own, :] = all_ref[base + channels : base + 2 * channels, :].astype(jnp.bfloat16)
        rest = all_ref[base + 2 * channels : base + 3 * channels, :]
        energy_ref[own, h * slices : (h + 1) * slices] = rest[:, :slices]
        ask_ref[h] = rest[:, slices : slices + channels]
        look_ref[h] = rest[:, slices + channels : slices + 2 * channels]
        content_ref[h] = rest[:, slices + 2 * channels : slices + 3 * channels]
        spot = slices + 3 * channels
        energy_ref[own, lanes + h : lanes + h + 1] = rest[:, spot : spot + 1]
    energy_high, energy_low = halves(energy_ref[...])
    logits_of = dot(energy_high, div_ref[...], TN) + dot(energy_low, div_ref[...], TN)
    pair_ref[...] = jnp.concatenate(halves(logits_of), axis=1)


def finish_kernel(
    in_ref, div_ref, part_ref, energy_ref, sharp_ref, scale_ref, premlp_ref, offset_ref
):
    local, channels, slices = energy_ref.shape
    unit = 2 * channels + 16
    div = []
    part = []
    for h in range(local):
        base = h * unit
        div.append(in_ref[base : base + channels, :])
        part.append(in_ref[base + channels : base + 2 * channels, :])
        tail = in_ref[base + 2 * channels : base + unit, :]
        tail = jnp.concatenate([tail[:, :128], tail[:, 128:]], axis=0)
        energy_ref[h] = tail[:, :slices]
        square = tail[:, slices : slices + channels]
        kept = jnp.where(same_head((channels, channels), 1, 1), square, 0.0)
        sharp_ref[0:1, h * channels : (h + 1) * channels] = jnp.sum(kept, axis=0, keepdims=True)
    div_ref[...] = jnp.concatenate(div, axis=0)
    part_ref[...] = jnp.concatenate(part, axis=0)
    base = local * unit
    scale_ref[...] = in_ref[base : base + 1, :]
    premlp_ref[...] = in_ref[base + 1 : base + 2, :]
    offset_ref[...] = in_ref[base + 2 : base + 3, :]


def norm_kernel(member_ref, x_ref, gain_ref, s_ref):
    x = x_ref[...].astype(jnp.float32)
    centered = x - jnp.mean(x, axis=1, keepdims=True)
    spread = jnp.mean(centered * centered, axis=1, keepdims=True)
    scaled = centered * lax.rsqrt(spread + NORM_EPS) * gain_ref[...]
    s_ref[...] = scaled.astype(jnp.bfloat16)


def front_kernel(
    s_ref,
    pair_ref,
    feat_ref,
    w_ref,
    m_ref,
    tot_ref,
    z_scr,
    r_scr,
    den_scr,
    *,
    heads,
    slices,
    chunk,
):
    step = pl.program_id(0)
    lanes = heads * slices

    @pl.when(step == 0)
    def _():
        m_ref[...] = jnp.zeros_like(m_ref)
        den_scr[...] = jnp.zeros_like(den_scr)

    scaled = s_ref[...]
    z_scr[...] = dot(pair_ref[...], jnp.concatenate([scaled, scaled], axis=1), NT)
    r_scr[...] = sharp_terms(z_scr[lanes : lanes + heads, :]) * (1.0 / SCORE_LIMIT)
    rows = s_ref.shape[0]
    for h in range(heads):
        span = slice(h * slices, (h + 1) * slices)
        for c in range(rows // chunk):
            cols = slice(c * chunk, (c + 1) * chunk)
            z = z_scr[span, cols] * r_scr[h : h + 1, cols]
            raised = jnp.exp(SCORE_LIMIT * jnp.tanh(z))
            weights = raised * (1.0 / jnp.sum(raised, axis=0, keepdims=True))
            w_ref[span, cols] = weights.astype(jnp.bfloat16)
            part = weights[:, 0:128]
            for k in range(1, chunk // 128):
                part = part + weights[:, k * 128 : (k + 1) * 128]
            den_scr[span, :] += part
    m_ref[...] += dot(w_ref[...], scaled)

    @pl.when(step == pl.num_programs(0) - 1)
    def _():
        full = dot_split(feat_ref[...], halves(m_ref[...]), NT)
        width = full.shape[0] // heads
        tot_ref[0:width, :] = fold_heads(full, heads, width, slices)
        ones = jnp.ones((8, 128), jnp.bfloat16)
        tot_ref[width : width + 8, :] = dot_split(ones, halves(den_scr[...]), NT)


def mixer_kernel(
    member_ref,
    x_ref,
    w_ref,
    loss_ref,
    gain_ref,
    expand_ref,
    expand_t_ref,
    offset_ref,
    contract_ref,
    contract_t_ref,
    token_ref,
    emit_ref,
    block_ref,
    back_ref,
    grads_ref,
    gains_ref,
    tg_ref,
    te_ref,
    acc_scr,
    wr_scr,
    gain_scr,
    *,
    heads,
    slices,
):
    step = pl.program_id(0)
    width = emit_ref.shape[0]

    @pl.when(step == 0)
    def _():
        te_ref[...] = dot(token_ref[...], emit_ref[...], TN).astype(jnp.bfloat16)
        acc_scr[...] = jnp.zeros_like(acc_scr)
        gain_scr[...] = jnp.zeros_like(gain_scr)
        wr_scr[...] = jnp.zeros_like(wr_scr)

    weights = w_ref[...]
    loss = loss_ref[...]
    residual = x_ref[...].astype(jnp.float32) + dot(weights, te_ref[...], TN)
    centered = residual - jnp.mean(residual, axis=1, keepdims=True)
    spread = jnp.mean(centered * centered, axis=1, keepdims=True)
    rstd = lax.rsqrt(spread + NORM_EPS)
    normal = centered * rstd
    gain = gain_ref[...]
    normed = (normal * gain).astype(jnp.bfloat16)
    inner = dot(normed, expand_ref[...]) + offset_ref[...]
    cubic = (GELU_CUBE * GELU_SCALE) * (inner * inner)
    half = 0.5 * jnp.tanh(inner * (GELU_SCALE + cubic)) + 0.5
    gelu = inner * half
    active = gelu.astype(jnp.bfloat16)
    slope = half + (gelu - gelu * half) * (2.0 * GELU_SCALE + 6.0 * cubic)
    block_ref[...] = (residual + dot(active, contract_ref[...])).astype(jnp.bfloat16)
    back_inner = dot(loss, contract_t_ref[...]) * slope
    back_low = back_inner.astype(jnp.bfloat16)
    back_normed = dot(back_low, expand_t_ref[...])
    pulled = back_normed * gain
    mean_pull = jnp.mean(pulled, axis=1, keepdims=True)
    mean_gain = jnp.mean(pulled * normal, axis=1, keepdims=True)
    back_resid = loss.astype(jnp.float32) + rstd * (pulled - mean_pull - normal * mean_gain)
    back = back_resid.astype(jnp.bfloat16)
    back_ref[...] = back
    acc_scr[0:width, :] += dot(normed, back_low, TN)
    acc_scr[width : 2 * width, :] += dot(active, loss, TN)
    rows = x_ref.shape[0]
    gain_scr[...] += jnp.sum(back_inner.reshape(rows // 8, 8, width), axis=0)
    wr_scr[...] += dot(weights, back)

    @pl.when(step == pl.num_programs(0) - 1)
    def _():
        pieces = halves(wr_scr[...])
        grads_ref[0:width, :] = dot_split(token_ref[...], pieces).astype(jnp.bfloat16)
        grads_ref[width : 3 * width, :] = acc_scr[...].astype(jnp.bfloat16)
        full = dot_split(emit_ref[...], pieces, NT)
        tg_ref[...] = fold_heads(full, heads, full.shape[0] // heads, slices)
        gains_ref[...] = jnp.zeros_like(gains_ref)
        product = halves(expand_ref[...].astype(jnp.float32) * acc_scr[0:width, :])
        total = dot_split(jnp.ones((8, product[0].shape[1]), jnp.bfloat16), product, NT)
        gains_ref[1:2, :] = total[0:1] / gain
        gains_ref[2:3, :] = jnp.sum(gain_scr[...], axis=0, keepdims=True)


def back_kernel(
    s_ref,
    back_ref,
    pair_ref,
    te_ref,
    den_ref,
    m_ref,
    energy_ref,
    num_ref,
    div_ref,
    part_ref,
    scale_ref,
    gains_ref,
    out_ref,
    z_scr,
    b_scr,
    r_scr,
    d_scr,
    g_scr,
    den_scr,
    tf_scr,
    *,
    heads,
    slices,
    chunk,
    local,
    block,
):
    step = pl.program_id(0)
    lanes = heads * slices

    @pl.when(step == 0)
    def _():
        g_scr[...] = jnp.zeros_like(g_scr)
        den_scr[...] = jnp.broadcast_to(den_ref[...], den_scr.shape)
        width = te_ref.shape[1]
        tf_scr[:, :width] = te_ref[...]
        tf_scr[:, width:] = dot(num_ref[...], part_ref[...], TN).astype(jnp.bfloat16)

    scaled = s_ref[...]
    z_scr[...] = dot(pair_ref[...], jnp.concatenate([scaled, scaled], axis=1), NT)
    b_scr[...] = dot(
        tf_scr[...],
        jnp.concatenate([back_ref[...], scaled], axis=1),
        NT,
    )
    raw = z_scr[lanes : lanes + heads, :]
    r_scr[...] = sharp_terms(raw)
    rows = s_ref.shape[0]
    for h in range(heads):
        span = slice(h * slices, (h + 1) * slices)
        for c in range(rows // chunk):
            cols = slice(c * chunk, (c + 1) * chunk)
            inverse = r_scr[h : h + 1, cols]
            z = z_scr[span, cols] * (inverse * (1.0 / SCORE_LIMIT))
            bent = jnp.tanh(z)
            raised = jnp.exp(SCORE_LIMIT * bent)
            weights = raised * (1.0 / jnp.sum(raised, axis=0, keepdims=True))
            back_w = b_scr[span, cols] + jnp.concatenate([den_scr[span, :]] * (chunk // 128), axis=1)
            middle = jnp.sum(weights * back_w, axis=0, keepdims=True)
            q = weights * (back_w - middle) * (1.0 - bent * bent)
            d_scr[span, cols] = (q * inverse).astype(jnp.bfloat16)
            z_scr[lanes + 8 + h : lanes + 9 + h, cols] = jnp.sum(q * z, axis=0, keepdims=True)
    pulled = z_scr[lanes + 8 : lanes + 8 + heads, :] * (-SCORE_LIMIT) * r_scr[...]
    pulled = pulled * (1.0 / (1.0 + jnp.exp(-raw)))
    pulled = jnp.concatenate([pulled, jnp.zeros((PAD - heads, rows), jnp.float32)], axis=0)
    d_scr[lanes : lanes + PAD, :] = pulled.astype(jnp.bfloat16)
    g_scr[...] += dot(d_scr[...], scaled)

    @pl.when(step == pl.num_programs(0) - 1)
    def _():
        grads = g_scr[...]
        div = div_ref[...].astype(jnp.float32)
        part = part_ref[...].astype(jnp.float32)
        pieces = halves(grads)
        energy_high, energy_low = halves(energy_ref[...])
        div_slope = dot_split(energy_high, pieces) + dot(energy_low, pieces[0])
        part_slope = dot_split(num_ref[...], halves(m_ref[...]))
        mixed = jnp.sum(div * div_slope + part * part_slope, axis=0, keepdims=True)
        mixed = mixed / scale_ref[...]
        full = dot_split(div_ref[...], pieces, NT)
        width = full.shape[0] // heads
        energy = fold_heads(full[:, :lanes], heads, width, slices)
        tail = full[:, lanes : lanes + PAD]
        sharp = jnp.where(same_head(tail.shape, width, 1), tail, 0.0)
        sharp = jnp.sum(sharp, axis=1, keepdims=True)
        unit = 2 * width + 16
        for h in range(heads):
            base = (h // local) * block + (h % local) * unit
            own = slice(h * width, (h + 1) * width)
            out_ref[base : base + width, :] = div_slope[own].astype(jnp.bfloat16)
            out_ref[base + width : base + 2 * width, :] = part_slope[own].astype(
                jnp.bfloat16
            )
            pair = jnp.concatenate(
                [
                    energy[:, h * slices : (h + 1) * slices],
                    jnp.broadcast_to(sharp[own], (width, 128 - slices)),
                ],
                axis=1,
            )
            out_ref[base + 2 * width : base + unit, :] = jnp.concatenate(
                [pair[:16], pair[16:]], axis=1
            ).astype(jnp.bfloat16)
        for g in range(heads // local):
            base = g * block + local * unit
            rows_left = block - local * unit
            tail = gains_ref[...] + jnp.where(
                lax.broadcasted_iota(jnp.int32, gains_ref.shape, 0) == 0, mixed, 0.0
            )
            if rows_left > 8:
                tail = jnp.concatenate(
                    [tail, jnp.zeros((rows_left - 8, mixed.shape[1]), jnp.float32)], axis=0
                )
            out_ref[base : base + rows_left, :] = tail.astype(jnp.bfloat16)


def cost(units, rows, width):
    return pl.CostEstimate(
        flops=2 * units * rows * width * width,
        transcendentals=4 * rows * width,
        bytes_accessed=units * rows * width,
    )


def whole(shape):
    return pl.BlockSpec(shape, lambda i, *refs: (0,) * len(shape))


def params():
    return pltpu.CompilerParams(
        dimension_semantics=("arbitrary",), vmem_limit_bytes=56 * 1024 * 1024
    )


def token_attention(total_num, total_den, asking_projection, lookup_projection, content_projection):
    tokens = total_num / (total_den[:, :, None] + NORM_EPS)
    query_rows = jnp.einsum("hse,hef->hsf", tokens, asking_projection, precision=HIGHEST)
    key_rows = jnp.einsum("hse,hef->hsf", tokens, lookup_projection, precision=HIGHEST)
    value_rows = jnp.einsum("hse,hef->hsf", tokens, content_projection, precision=HIGHEST)
    scores = (
        jnp.einsum("hsf,htf->hst", query_rows, key_rows, precision=HIGHEST)
        * query_rows.shape[-1] ** (-0.5)
    )
    bounded_energies = SCORE_LIMIT * jnp.tanh(scores / SCORE_LIMIT)
    raised = jnp.exp(bounded_energies)
    attend = raised / jnp.sum(raised, axis=-1, keepdims=True)
    return jnp.einsum("hst,htf->hsf", attend, value_rows, precision=HIGHEST)


def block_diagonal(value):
    heads, rows, columns = value.shape
    eye = jnp.eye(heads, dtype=value.dtype)
    return (value[:, :, None, :] * eye[:, None, :, None]).reshape(heads * rows, heads * columns)


def body(
    mesh_signals,
    loss_sensitivity,
    divider_projection,
    partition_projection,
    sharpness_axis,
    partition_energies,
    asking_projection,
    lookup_projection,
    content_projection,
    prefocus_scale,
    emit_projection,
    premlp_scale,
    expand_factor,
    expand_offset,
    contract_factor,
):
    groups = lax.axis_size("head")
    member = lax.axis_index("head")
    rows = loss_sensitivity.shape[0]
    width = mesh_signals.shape[1]
    local, channels, slices = partition_energies.shape
    heads = local * groups
    lanes = heads * slices
    every_group = axis_groups("pts") + axis_groups("head")
    place = member.reshape(1).astype(jnp.int32)

    packed = pl.pallas_call(
        pack_kernel,
        out_shape=jax.ShapeDtypeStruct((groups, 3 * local * channels, width), jnp.float32),
        name="pack",
    )(
        divider_projection.T,
        partition_projection.T,
        sharpness_axis[None, :],
        partition_energies,
        asking_projection,
        lookup_projection,
        content_projection,
    )
    packed = lax.all_to_all(packed, "head", 0, 0, tiled=True)
    packed = packed.reshape(3 * heads * channels, width)
    square = jax.ShapeDtypeStruct((heads, channels, channels), jnp.float32)
    pair, energy_rows, div_t, part_t, asking, lookup, content = pl.pallas_call(
        unpack_kernel,
        out_shape=[
            jax.ShapeDtypeStruct((lanes + PAD, 2 * width), jnp.bfloat16),
            jax.ShapeDtypeStruct((heads * channels, lanes + PAD), jnp.float32),
            jax.ShapeDtypeStruct((heads * channels, width), jnp.bfloat16),
            jax.ShapeDtypeStruct((heads * channels, width), jnp.bfloat16),
            square,
            square,
            square,
        ],
        name="unpack",
    )(packed)

    tile = 2048
    steps = rows // tile
    total_rows = lanes + PAD
    row_block = pl.BlockSpec((tile, width), lambda i, *refs: (i, 0))
    own_block = pl.BlockSpec((tile, width), lambda i, place: (place[0] * steps + i, 0))
    column_block = pl.BlockSpec((lanes, tile), lambda i, *refs: (0, i))
    scaled = pl.pallas_call(
        norm_kernel,
        grid_spec=pltpu.PrefetchScalarGridSpec(
            num_scalar_prefetch=1,
            grid=(steps,),
            in_specs=[own_block, whole((1, width))],
            out_specs=row_block,
        ),
        out_shape=jax.ShapeDtypeStruct((rows, width), jnp.bfloat16),
        compiler_params=params(),
        cost_estimate=cost(8, rows, width),
        name="norm",
    )(place, mesh_signals, prefocus_scale[None, :])
    weights, moment, totals = pl.pallas_call(
        functools.partial(front_kernel, heads=heads, slices=slices, chunk=256),
        grid=(steps,),
        in_specs=[
            row_block,
            whole((total_rows, 2 * width)),
            whole((heads * channels, width)),
        ],
        out_specs=[
            column_block,
            whole((lanes, width)),
            whole((channels + 8, lanes)),
        ],
        scratch_shapes=[
            pltpu.VMEM((total_rows, tile), jnp.float32),
            pltpu.VMEM((heads, tile), jnp.float32),
            pltpu.VMEM((lanes, 128), jnp.float32),
        ],
        out_shape=[
            jax.ShapeDtypeStruct((lanes, rows), jnp.bfloat16),
            jax.ShapeDtypeStruct((lanes, width), jnp.float32),
            jax.ShapeDtypeStruct((channels + 8, lanes), jnp.float32),
        ],
        compiler_params=params(),
        cost_estimate=cost(16, rows, width),
        name="front",
    )(scaled, pair, part_t)

    totals = all_sum(totals, every_group)
    total_num = totals[:channels].reshape(channels, heads, slices).transpose(1, 2, 0)
    total_den = totals[channels].reshape(heads, slices)
    token_out, token_back = jax.vjp(
        token_attention, total_num, total_den, asking, lookup, content
    )
    token_low = token_out.astype(jnp.bfloat16)
    token_rows = block_diagonal(token_low.transpose(0, 2, 1))

    block_result, back_low, grads, gains, token_grad, token_emit = pl.pallas_call(
        functools.partial(mixer_kernel, heads=heads, slices=slices),
        grid_spec=pltpu.PrefetchScalarGridSpec(
            num_scalar_prefetch=1,
            grid=(steps,),
            in_specs=[
                own_block,
                column_block,
                row_block,
                whole((1, width)),
                whole(expand_factor.shape),
                whole(expand_factor.shape[::-1]),
                whole((1, expand_offset.shape[0])),
                whole(contract_factor.shape),
                whole(contract_factor.shape[::-1]),
                whole(token_rows.shape),
                whole(emit_projection.shape),
            ],
            out_specs=[
                row_block,
                row_block,
                whole((3 * width, width)),
                whole((8, width)),
                whole((channels, lanes)),
                whole((lanes, width)),
            ],
            scratch_shapes=[
                pltpu.VMEM((2 * width, width), jnp.float32),
                pltpu.VMEM((lanes, width), jnp.float32),
                pltpu.VMEM((8, width), jnp.float32),
            ],
        ),
        out_shape=[
            jax.ShapeDtypeStruct((rows, width), jnp.bfloat16),
            jax.ShapeDtypeStruct((rows, width), jnp.bfloat16),
            jax.ShapeDtypeStruct((3 * width, width), jnp.bfloat16),
            jax.ShapeDtypeStruct((8, width), jnp.float32),
            jax.ShapeDtypeStruct((channels, lanes), jnp.float32),
            jax.ShapeDtypeStruct((lanes, width), jnp.bfloat16),
        ],
        compiler_params=params(),
        cost_estimate=cost(26, rows, width),
        name="mixer",
    )(
        place,
        mesh_signals,
        weights,
        loss_sensitivity,
        premlp_scale[None, :],
        expand_factor,
        expand_factor.T,
        expand_offset[None, :],
        contract_factor,
        contract_factor.T,
        token_rows,
        emit_projection,
    )

    for group in every_group:
        token_grad = group_sum(token_grad, group)
    token_grad = token_grad.reshape(channels, heads, slices).transpose(1, 2, 0)
    back_num, back_den, asking_slope, lookup_slope, content_slope = token_back(token_grad)
    num_low = block_diagonal(back_num.astype(jnp.bfloat16).transpose(0, 2, 1))
    den_rows = back_den.reshape(lanes, 1)

    everyone = ("head", "pts")
    grads = exchange_sum(grads, everyone)
    grads = gather(grads.astype(jnp.bfloat16), everyone).astype(jnp.float32)

    unit = 2 * channels + 16
    grain = 8 * lax.axis_size("pts")
    block = -(-(local * unit + 8) // grain) * grain
    back_call = pl.pallas_call(
        functools.partial(back_kernel, heads=heads, slices=slices, chunk=256, local=local, block=block),
        grid=(steps,),
        in_specs=[
            row_block,
            row_block,
            whole((total_rows, 2 * width)),
            whole((lanes, width)),
            whole((lanes, 1)),
            whole((lanes, width)),
            whole((heads * channels, total_rows)),
            whole((heads * channels, lanes)),
            whole((heads * channels, width)),
            whole((heads * channels, width)),
            whole((1, width)),
            whole((8, width)),
        ],
        out_specs=whole((groups * block, width)),
        scratch_shapes=[
            pltpu.VMEM((total_rows, tile), jnp.float32),
            pltpu.VMEM((lanes, tile), jnp.float32),
            pltpu.VMEM((heads, tile), jnp.float32),
            pltpu.VMEM((total_rows, tile), jnp.bfloat16),
            pltpu.VMEM((total_rows, width), jnp.float32),
            pltpu.VMEM((lanes, 128), jnp.float32),
            pltpu.VMEM((lanes, 2 * width), jnp.bfloat16),
        ],
        out_shape=jax.ShapeDtypeStruct((groups * block, width), jnp.bfloat16),
        compiler_params=params(),
        cost_estimate=cost(26, rows, width),
        name="back",
    )
    head_grads = back_call(
        scaled,
        back_low,
        pair,
        token_emit,
        den_rows,
        moment,
        energy_rows,
        num_low,
        div_t,
        part_t,
        prefocus_scale[None, :],
        gains,
    )

    head_grads, grads = lax.optimization_barrier((head_grads, grads))
    head_grads = gather(exchange_sum(head_grads, everyone), ("pts",))
    row = jax.ShapeDtypeStruct((1, width), jnp.float32)
    flat = jax.ShapeDtypeStruct((local * channels, width), jnp.float32)
    divider_slope, partition_slope, energy_slope, sharp_slope, scale_slope, premlp_slope, offset_slope = (
        pl.pallas_call(
            finish_kernel,
            out_shape=[
                flat,
                flat,
                jax.ShapeDtypeStruct((local, channels, slices), jnp.float32),
                jax.ShapeDtypeStruct((1, local * channels), jnp.float32),
                row,
                row,
                row,
            ],
            name="finish",
        )(head_grads)
    )

    def own_heads(value):
        return lax.dynamic_slice_in_dim(value, member * local, local, 0)

    return (
        block_result,
        divider_slope.T,
        partition_slope.T,
        sharp_slope.reshape(-1),
        energy_slope,
        own_heads(asking_slope),
        own_heads(lookup_slope),
        own_heads(content_slope),
        scale_slope.reshape(-1),
        grads[:width],
        premlp_slope.reshape(-1),
        grads[width : 2 * width],
        offset_slope.reshape(-1),
        grads[2 * width : 3 * width],
    )


def solution(mesh):
    in_specs = (
        P("pts", None),
        P(("pts", "head"), None),
        P(None, "head"),
        P(None, "head"),
        P("head"),
        P("head", None, None),
        P("head", None, None),
        P("head", None, None),
        P("head", None, None),
        P(),
        P(),
        P(),
        P(),
        P(),
        P(),
    )
    out_specs = (
        P(("pts", "head"), None),
        P(None, "head"),
        P(None, "head"),
        P("head"),
        P("head", None, None),
        P("head", None, None),
        P("head", None, None),
        P("head", None, None),
        P(),
        P(),
        P(),
        P(),
        P(),
        P(),
    )
    return jax.shard_map(body, mesh=mesh, in_specs=in_specs, out_specs=out_specs, check_vma=False)
```

```python
import functools

import jax
import jax.numpy as jnp
from jax import lax
from jax.experimental import pallas as pl
from jax.experimental.pallas import tpu as pltpu
from jax.sharding import PartitionSpec as P


SCORE_LIMIT = 30.0
NORM_EPS = 1e-05
GELU_SCALE = 0.7978845608028654
GELU_CUBE = 0.044715
HIGHEST = lax.Precision.HIGHEST
PAD = 16


NN = (((1,), (0,)), ((), ()))
NT = (((1,), (1,)), ((), ()))
TN = (((0,), (0,)), ((), ()))


def dot(a, b, numbers=NN, precision=None):
    return lax.dot_general(a, b, numbers, precision=precision, preferred_element_type=jnp.float32)


def halves(value):
    high = value.astype(jnp.bfloat16)
    return high, (value - high.astype(jnp.float32)).astype(jnp.bfloat16)


def dot_split(a, b, numbers=NN):
    return dot(a, b[0], numbers) + dot(a, b[1], numbers)


def axis_groups(axis):
    size = lax.axis_size(axis)
    groups = []
    stride = 1
    step = 2 if axis == "pts" else 4
    while stride < size:
        count = min(step, size // stride)
        groups.append((axis, stride, count))
        stride *= count
        step = 4
    return groups


def swap(value, axis, distance):
    size = lax.axis_size(axis)
    return lax.ppermute(value, axis, [(i, i ^ distance) for i in range(size)])


def tree_sum(parts):
    while len(parts) > 1:
        parts = [parts[i] + parts[i + 1] for i in range(0, len(parts), 2)]
    return parts[0]


def group_sum(value, group):
    axis, stride, count = group
    return tree_sum([value] + [swap(value, axis, m * stride) for m in range(1, count)])


def all_sum(value, groups):
    for group in groups:
        value = group_sum(value, group)
    return value


def exchange_sum(value, axes):
    count = 1
    for axis in axes:
        count *= lax.axis_size(axis)
    block = value.shape[0] // count
    pieces = lax.all_to_all(value.reshape(count, block, value.shape[1]), axes, 0, 0, tiled=True)
    return jnp.sum(pieces.astype(jnp.float32), axis=0)


def gather(value, axes):
    count = 1
    for axis in axes:
        count *= lax.axis_size(axis)
    full = lax.all_to_all(
        jnp.broadcast_to(value[None], (count,) + value.shape), axes, 0, 0, tiled=True
    )
    return full.reshape((count * value.shape[0],) + value.shape[1:])


def same_head(shape, row_span, column_span):
    rows = lax.broadcasted_iota(jnp.int32, shape, 0) // row_span
    columns = lax.broadcasted_iota(jnp.int32, shape, 1) // column_span
    return rows == columns


def fold_heads(full, heads, width, slices):
    kept = jnp.where(same_head(full.shape, width, slices), full, 0.0)
    return jnp.sum(kept.reshape(heads, width, heads * slices), axis=0)


def sharp_terms(raw):
    sharpness = 0.5 + jnp.maximum(raw, 0.0) + jnp.log1p(jnp.exp(-jnp.abs(raw)))
    return 1.0 / sharpness


def spread_column(row):
    count = row.shape[1]
    square = jnp.broadcast_to(row, (count, count))
    return jnp.sum(jnp.where(same_head((count, count), 1, 1), square, 0.0), axis=1, keepdims=True)


def pack_kernel(div_ref, part_ref, sharp_ref, energy_ref, ask_ref, look_ref, content_ref, out_ref):
    local, channels, slices = energy_ref.shape
    copies, _, width = out_ref.shape
    div = div_ref[...].astype(jnp.float32)
    part = part_ref[...].astype(jnp.float32)
    for h in range(local):
        base = 3 * channels * h
        own = slice(h * channels, (h + 1) * channels)
        sharp = spread_column(sharp_ref[0:1, own])
        rest = jnp.concatenate(
            [
                energy_ref[h],
                ask_ref[h],
                look_ref[h],
                content_ref[h],
                jnp.broadcast_to(sharp, (channels, width - slices - 3 * channels)),
            ],
            axis=1,
        )
        for g in range(copies):
            out_ref[g, base : base + channels, :] = div[own]
            out_ref[g, base + channels : base + 2 * channels, :] = part[own]
            out_ref[g, base + 2 * channels : base + 3 * channels, :] = rest


def unpack_kernel(
    all_ref, pair_ref, energy_ref, div_ref, part_ref, ask_ref, look_ref, content_ref
):
    heads, channels, _ = ask_ref.shape
    lanes = pair_ref.shape[0] - PAD
    slices = lanes // heads
    energy_ref[...] = jnp.zeros_like(energy_ref)
    for h in range(heads):
        base = 3 * channels * h
        own = slice(h * channels, (h + 1) * channels)
        div_ref[own, :] = all_ref[base : base + channels, :].astype(jnp.bfloat16)
        part_ref[own, :] = all_ref[base + channels : base + 2 * channels, :].astype(jnp.bfloat16)
        rest = all_ref[base + 2 * channels : base + 3 * channels, :]
        energy_ref[own, h * slices : (h + 1) * slices] = rest[:, :slices]
        ask_ref[h] = rest[:, slices : slices + channels]
        look_ref[h] = rest[:, slices + channels : slices + 2 * channels]
        content_ref[h] = rest[:, slices + 2 * channels : slices + 3 * channels]
        spot = slices + 3 * channels
        energy_ref[own, lanes + h : lanes + h + 1] = rest[:, spot : spot + 1]
    energy_high, energy_low = halves(energy_ref[...])
    logits_of = dot(energy_high, div_ref[...], TN) + dot(energy_low, div_ref[...], TN)
    pair_ref[...] = jnp.concatenate(halves(logits_of), axis=1)


def finish_kernel(
    in_ref, div_ref, part_ref, energy_ref, sharp_ref, scale_ref, premlp_ref, offset_ref
):
    local, channels, slices = energy_ref.shape
    unit = 2 * channels + 16
    values = in_ref[...].astype(jnp.float32)
    div = []
    part = []
    for h in range(local):
        base = h * unit
        div.append(values[base : base + channels, :])
        part.append(values[base + channels : base + 2 * channels, :])
        tail = values[base + 2 * channels : base + unit, :]
        tail = jnp.concatenate([tail[:, :128], tail[:, 128:]], axis=0)
        energy_ref[h] = tail[:, :slices]
        square = tail[:, slices : slices + channels]
        kept = jnp.where(same_head((channels, channels), 1, 1), square, 0.0)
        sharp_ref[0:1, h * channels : (h + 1) * channels] = jnp.sum(kept, axis=0, keepdims=True)
    div_ref[...] = jnp.concatenate(div, axis=0)
    part_ref[...] = jnp.concatenate(part, axis=0)
    base = local * unit
    scale_ref[...] = values[base : base + 1, :]
    premlp_ref[...] = values[base + 1 : base + 2, :]
    offset_ref[...] = values[base + 2 : base + 3, :]


def norm_kernel(member_ref, x_ref, gain_ref, s_ref):
    x = x_ref[...].astype(jnp.float32)
    centered = x - jnp.mean(x, axis=1, keepdims=True)
    spread = jnp.mean(centered * centered, axis=1, keepdims=True)
    scaled = centered * lax.rsqrt(spread + NORM_EPS) * gain_ref[...]
    s_ref[...] = scaled.astype(jnp.bfloat16)


def front_kernel(
    s_ref,
    pair_ref,
    feat_ref,
    w_ref,
    m_ref,
    tot_ref,
    z_scr,
    r_scr,
    den_scr,
    *,
    heads,
    slices,
    chunk,
):
    step = pl.program_id(0)
    lanes = heads * slices

    @pl.when(step == 0)
    def _():
        m_ref[...] = jnp.zeros_like(m_ref)
        den_scr[...] = jnp.zeros_like(den_scr)

    scaled = s_ref[...]
    z_scr[...] = dot(pair_ref[...], jnp.concatenate([scaled, scaled], axis=1), NT)
    r_scr[...] = sharp_terms(z_scr[lanes : lanes + heads, :]) * (1.0 / SCORE_LIMIT)
    rows = s_ref.shape[0]
    for h in range(heads):
        span = slice(h * slices, (h + 1) * slices)
        for c in range(rows // chunk):
            cols = slice(c * chunk, (c + 1) * chunk)
            z = z_scr[span, cols] * r_scr[h : h + 1, cols]
            raised = jnp.exp(SCORE_LIMIT * jnp.tanh(z))
            weights = raised * (1.0 / jnp.sum(raised, axis=0, keepdims=True))
            w_ref[span, cols] = weights.astype(jnp.bfloat16)
            part = weights[:, 0:128]
            for k in range(1, chunk // 128):
                part = part + weights[:, k * 128 : (k + 1) * 128]
            den_scr[span, :] += part
    m_ref[...] += dot(w_ref[...], scaled)

    @pl.when(step == pl.num_programs(0) - 1)
    def _():
        full = dot_split(feat_ref[...], halves(m_ref[...]), NT)
        width = full.shape[0] // heads
        tot_ref[0:width, :] = fold_heads(full, heads, width, slices)
        ones = jnp.ones((8, 128), jnp.bfloat16)
        tot_ref[width : width + 8, :] = dot_split(ones, halves(den_scr[...]), NT)


def mixer_kernel(
    member_ref,
    x_ref,
    w_ref,
    loss_ref,
    gain_ref,
    expand_ref,
    expand_t_ref,
    offset_ref,
    contract_ref,
    contract_t_ref,
    token_ref,
    emit_ref,
    block_ref,
    back_ref,
    grads_ref,
    gains_ref,
    tg_ref,
    te_ref,
    acc_scr,
    wr_scr,
    gain_scr,
    *,
    heads,
    slices,
):
    step = pl.program_id(0)
    width = emit_ref.shape[0]

    @pl.when(step == 0)
    def _():
        te_ref[...] = dot(token_ref[...], emit_ref[...], TN).astype(jnp.bfloat16)
        acc_scr[...] = jnp.zeros_like(acc_scr)
        gain_scr[...] = jnp.zeros_like(gain_scr)
        wr_scr[...] = jnp.zeros_like(wr_scr)

    weights = w_ref[...]
    loss = loss_ref[...]
    residual = x_ref[...].astype(jnp.float32) + dot(weights, te_ref[...], TN)
    centered = residual - jnp.mean(residual, axis=1, keepdims=True)
    spread = jnp.mean(centered * centered, axis=1, keepdims=True)
    rstd = lax.rsqrt(spread + NORM_EPS)
    normal = centered * rstd
    gain = gain_ref[...]
    normed = (normal * gain).astype(jnp.bfloat16)
    inner = dot(normed, expand_ref[...]) + offset_ref[...]
    cubic = (GELU_CUBE * GELU_SCALE) * (inner * inner)
    half = 0.5 * jnp.tanh(inner * (GELU_SCALE + cubic)) + 0.5
    gelu = inner * half
    active = gelu.astype(jnp.bfloat16)
    slope = half + (gelu - gelu * half) * (2.0 * GELU_SCALE + 6.0 * cubic)
    block_ref[...] = (residual + dot(active, contract_ref[...])).astype(jnp.bfloat16)
    back_inner = dot(loss, contract_t_ref[...]) * slope
    back_low = back_inner.astype(jnp.bfloat16)
    back_normed = dot(back_low, expand_t_ref[...])
    pulled = back_normed * gain
    mean_pull = jnp.mean(pulled, axis=1, keepdims=True)
    mean_gain = jnp.mean(pulled * normal, axis=1, keepdims=True)
    back_resid = loss.astype(jnp.float32) + rstd * (pulled - mean_pull - normal * mean_gain)
    back = back_resid.astype(jnp.bfloat16)
    back_ref[...] = back
    acc_scr[0:width, :] += dot(normed, back_low, TN)
    acc_scr[width : 2 * width, :] += dot(active, loss, TN)
    rows = x_ref.shape[0]
    gain_scr[...] += jnp.sum(back_inner.reshape(rows // 8, 8, width), axis=0)
    wr_scr[...] += dot(weights, back)

    @pl.when(step == pl.num_programs(0) - 1)
    def _():
        pieces = halves(wr_scr[...])
        grads_ref[0:width, :] = dot_split(token_ref[...], pieces).astype(jnp.bfloat16)
        grads_ref[width : 3 * width, :] = acc_scr[...].astype(jnp.bfloat16)
        full = dot_split(emit_ref[...], pieces, NT)
        tg_ref[...] = fold_heads(full, heads, full.shape[0] // heads, slices)
        gains_ref[...] = jnp.zeros_like(gains_ref)
        product = halves(expand_ref[...].astype(jnp.float32) * acc_scr[0:width, :])
        total = dot_split(jnp.ones((8, product[0].shape[1]), jnp.bfloat16), product, NT)
        gains_ref[1:2, :] = total[0:1] / gain
        gains_ref[2:3, :] = jnp.sum(gain_scr[...], axis=0, keepdims=True)


def back_kernel(
    s_ref,
    back_ref,
    pair_ref,
    te_ref,
    den_ref,
    m_ref,
    energy_ref,
    num_ref,
    div_ref,
    part_ref,
    scale_ref,
    gains_ref,
    out_ref,
    z_scr,
    b_scr,
    r_scr,
    d_scr,
    g_scr,
    den_scr,
    tf_scr,
    *,
    heads,
    slices,
    chunk,
    local,
    block,
):
    step = pl.program_id(0)
    lanes = heads * slices

    @pl.when(step == 0)
    def _():
        g_scr[...] = jnp.zeros_like(g_scr)
        den_scr[...] = jnp.broadcast_to(den_ref[...], den_scr.shape)
        width = te_ref.shape[1]
        tf_scr[:, :width] = te_ref[...]
        tf_scr[:, width:] = dot(num_ref[...], part_ref[...], TN).astype(jnp.bfloat16)

    scaled = s_ref[...]
    z_scr[...] = dot(pair_ref[...], jnp.concatenate([scaled, scaled], axis=1), NT)
    b_scr[...] = dot(
        tf_scr[...],
        jnp.concatenate([back_ref[...], scaled], axis=1),
        NT,
    )
    raw = z_scr[lanes : lanes + heads, :]
    r_scr[...] = sharp_terms(raw)
    rows = s_ref.shape[0]
    for h in range(heads):
        span = slice(h * slices, (h + 1) * slices)
        for c in range(rows // chunk):
            cols = slice(c * chunk, (c + 1) * chunk)
            inverse = r_scr[h : h + 1, cols]
            z = z_scr[span, cols] * (inverse * (1.0 / SCORE_LIMIT))
            bent = jnp.tanh(z)
            raised = jnp.exp(SCORE_LIMIT * bent)
            weights = raised * (1.0 / jnp.sum(raised, axis=0, keepdims=True))
            back_w = b_scr[span, cols] + jnp.concatenate([den_scr[span, :]] * (chunk // 128), axis=1)
            middle = jnp.sum(weights * back_w, axis=0, keepdims=True)
            q = weights * (back_w - middle) * (1.0 - bent * bent)
            d_scr[span, cols] = (q * inverse).astype(jnp.bfloat16)
            z_scr[lanes + 8 + h : lanes + 9 + h, cols] = jnp.sum(q * z, axis=0, keepdims=True)
    pulled = z_scr[lanes + 8 : lanes + 8 + heads, :] * (-SCORE_LIMIT) * r_scr[...]
    pulled = pulled * (1.0 / (1.0 + jnp.exp(-raw)))
    pulled = jnp.concatenate([pulled, jnp.zeros((PAD - heads, rows), jnp.float32)], axis=0)
    d_scr[lanes : lanes + PAD, :] = pulled.astype(jnp.bfloat16)
    g_scr[...] += dot(d_scr[...], scaled)

    @pl.when(step == pl.num_programs(0) - 1)
    def _():
        grads = g_scr[...]
        div = div_ref[...].astype(jnp.float32)
        part = part_ref[...].astype(jnp.float32)
        pieces = halves(grads)
        energy_high, energy_low = halves(energy_ref[...])
        div_slope = dot_split(energy_high, pieces) + dot(energy_low, pieces[0])
        part_slope = dot_split(num_ref[...], halves(m_ref[...]))
        mixed = jnp.sum(div * div_slope + part * part_slope, axis=0, keepdims=True)
        mixed = mixed / scale_ref[...]
        full = dot_split(div_ref[...], pieces, NT)
        width = full.shape[0] // heads
        energy = fold_heads(full[:, :lanes], heads, width, slices)
        tail = full[:, lanes : lanes + PAD]
        sharp = jnp.where(same_head(tail.shape, width, 1), tail, 0.0)
        sharp = jnp.sum(sharp, axis=1, keepdims=True)
        unit = 2 * width + 16
        for h in range(heads):
            base = (h // local) * block + (h % local) * unit
            own = slice(h * width, (h + 1) * width)
            out_ref[base : base + width, :] = div_slope[own].astype(jnp.bfloat16)
            out_ref[base + width : base + 2 * width, :] = part_slope[own].astype(
                jnp.bfloat16
            )
            pair = jnp.concatenate(
                [
                    energy[:, h * slices : (h + 1) * slices],
                    jnp.broadcast_to(sharp[own], (width, 128 - slices)),
                ],
                axis=1,
            )
            out_ref[base + 2 * width : base + unit, :] = jnp.concatenate(
                [pair[:16], pair[16:]], axis=1
            ).astype(jnp.bfloat16)
        for g in range(heads // local):
            base = g * block + local * unit
            rows_left = block - local * unit
            tail = gains_ref[...] + jnp.where(
                lax.broadcasted_iota(jnp.int32, gains_ref.shape, 0) == 0, mixed, 0.0
            )
            if rows_left > 8:
                tail = jnp.concatenate(
                    [tail, jnp.zeros((rows_left - 8, mixed.shape[1]), jnp.float32)], axis=0
                )
            out_ref[base : base + rows_left, :] = tail.astype(jnp.bfloat16)


def cost(units, rows, width):
    return pl.CostEstimate(
        flops=2 * units * rows * width * width,
        transcendentals=4 * rows * width,
        bytes_accessed=units * rows * width,
    )


def whole(shape):
    return pl.BlockSpec(shape, lambda i, *refs: (0,) * len(shape))


def params():
    return pltpu.CompilerParams(
        dimension_semantics=("arbitrary",), vmem_limit_bytes=56 * 1024 * 1024
    )


def token_attention(total_num, total_den, asking_projection, lookup_projection, content_projection):
    tokens = total_num / (total_den[:, :, None] + NORM_EPS)
    query_rows = jnp.einsum("hse,hef->hsf", tokens, asking_projection, precision=HIGHEST)
    key_rows = jnp.einsum("hse,hef->hsf", tokens, lookup_projection, precision=HIGHEST)
    value_rows = jnp.einsum("hse,hef->hsf", tokens, content_projection, precision=HIGHEST)
    scores = (
        jnp.einsum("hsf,htf->hst", query_rows, key_rows, precision=HIGHEST)
        * query_rows.shape[-1] ** (-0.5)
    )
    bounded_energies = SCORE_LIMIT * jnp.tanh(scores / SCORE_LIMIT)
    raised = jnp.exp(bounded_energies)
    attend = raised / jnp.sum(raised, axis=-1, keepdims=True)
    return jnp.einsum("hst,htf->hsf", attend, value_rows, precision=HIGHEST)


def block_diagonal(value):
    heads, rows, columns = value.shape
    eye = jnp.eye(heads, dtype=value.dtype)
    return (value[:, :, None, :] * eye[:, None, :, None]).reshape(heads * rows, heads * columns)


def body(
    mesh_signals,
    loss_sensitivity,
    divider_projection,
    partition_projection,
    sharpness_axis,
    partition_energies,
    asking_projection,
    lookup_projection,
    content_projection,
    prefocus_scale,
    emit_projection,
    premlp_scale,
    expand_factor,
    expand_offset,
    contract_factor,
):
    groups = lax.axis_size("head")
    member = lax.axis_index("head")
    rows = loss_sensitivity.shape[0]
    width = mesh_signals.shape[1]
    local, channels, slices = partition_energies.shape
    heads = local * groups
    lanes = heads * slices
    every_group = axis_groups("pts") + axis_groups("head")
    place = member.reshape(1).astype(jnp.int32)

    packed = pl.pallas_call(
        pack_kernel,
        out_shape=jax.ShapeDtypeStruct((groups, 3 * local * channels, width), jnp.float32),
        name="pack",
    )(
        divider_projection.T,
        partition_projection.T,
        sharpness_axis[None, :],
        partition_energies,
        asking_projection,
        lookup_projection,
        content_projection,
    )
    packed = lax.all_to_all(packed, "head", 0, 0, tiled=True)
    packed = packed.reshape(3 * heads * channels, width)
    square = jax.ShapeDtypeStruct((heads, channels, channels), jnp.float32)
    pair, energy_rows, div_t, part_t, asking, lookup, content = pl.pallas_call(
        unpack_kernel,
        out_shape=[
            jax.ShapeDtypeStruct((lanes + PAD, 2 * width), jnp.bfloat16),
            jax.ShapeDtypeStruct((heads * channels, lanes + PAD), jnp.float32),
            jax.ShapeDtypeStruct((heads * channels, width), jnp.bfloat16),
            jax.ShapeDtypeStruct((heads * channels, width), jnp.bfloat16),
            square,
            square,
            square,
        ],
        name="unpack",
    )(packed)

    tile = 2048
    steps = rows // tile
    total_rows = lanes + PAD
    row_block = pl.BlockSpec((tile, width), lambda i, *refs: (i, 0))
    own_block = pl.BlockSpec((tile, width), lambda i, place: (place[0] * steps + i, 0))
    column_block = pl.BlockSpec((lanes, tile), lambda i, *refs: (0, i))
    scaled = pl.pallas_call(
        norm_kernel,
        grid_spec=pltpu.PrefetchScalarGridSpec(
            num_scalar_prefetch=1,
            grid=(steps,),
            in_specs=[own_block, whole((1, width))],
            out_specs=row_block,
        ),
        out_shape=jax.ShapeDtypeStruct((rows, width), jnp.bfloat16),
        compiler_params=params(),
        cost_estimate=cost(8, rows, width),
        name="norm",
    )(place, mesh_signals, prefocus_scale[None, :])
    weights, moment, totals = pl.pallas_call(
        functools.partial(front_kernel, heads=heads, slices=slices, chunk=256),
        grid=(steps,),
        in_specs=[
            row_block,
            whole((total_rows, 2 * width)),
            whole((heads * channels, width)),
        ],
        out_specs=[
            column_block,
            whole((lanes, width)),
            whole((channels + 8, lanes)),
        ],
        scratch_shapes=[
            pltpu.VMEM((total_rows, tile), jnp.float32),
            pltpu.VMEM((heads, tile), jnp.float32),
            pltpu.VMEM((lanes, 128), jnp.float32),
        ],
        out_shape=[
            jax.ShapeDtypeStruct((lanes, rows), jnp.bfloat16),
            jax.ShapeDtypeStruct((lanes, width), jnp.float32),
            jax.ShapeDtypeStruct((channels + 8, lanes), jnp.float32),
        ],
        compiler_params=params(),
        cost_estimate=cost(16, rows, width),
        name="front",
    )(scaled, pair, part_t)

    totals = all_sum(totals, every_group)
    total_num = totals[:channels].reshape(channels, heads, slices).transpose(1, 2, 0)
    total_den = totals[channels].reshape(heads, slices)
    token_out, token_back = jax.vjp(
        token_attention, total_num, total_den, asking, lookup, content
    )
    token_low = token_out.astype(jnp.bfloat16)
    token_rows = block_diagonal(token_low.transpose(0, 2, 1))

    block_result, back_low, grads, gains, token_grad, token_emit = pl.pallas_call(
        functools.partial(mixer_kernel, heads=heads, slices=slices),
        grid_spec=pltpu.PrefetchScalarGridSpec(
            num_scalar_prefetch=1,
            grid=(steps,),
            in_specs=[
                own_block,
                column_block,
                row_block,
                whole((1, width)),
                whole(expand_factor.shape),
                whole(expand_factor.shape[::-1]),
                whole((1, expand_offset.shape[0])),
                whole(contract_factor.shape),
                whole(contract_factor.shape[::-1]),
                whole(token_rows.shape),
                whole(emit_projection.shape),
            ],
            out_specs=[
                row_block,
                row_block,
                whole((3 * width, width)),
                whole((8, width)),
                whole((channels, lanes)),
                whole((lanes, width)),
            ],
            scratch_shapes=[
                pltpu.VMEM((2 * width, width), jnp.float32),
                pltpu.VMEM((lanes, width), jnp.float32),
                pltpu.VMEM((8, width), jnp.float32),
            ],
        ),
        out_shape=[
            jax.ShapeDtypeStruct((rows, width), jnp.bfloat16),
            jax.ShapeDtypeStruct((rows, width), jnp.bfloat16),
            jax.ShapeDtypeStruct((3 * width, width), jnp.bfloat16),
            jax.ShapeDtypeStruct((8, width), jnp.float32),
            jax.ShapeDtypeStruct((channels, lanes), jnp.float32),
            jax.ShapeDtypeStruct((lanes, width), jnp.bfloat16),
        ],
        compiler_params=params(),
        cost_estimate=cost(26, rows, width),
        name="mixer",
    )(
        place,
        mesh_signals,
        weights,
        loss_sensitivity,
        premlp_scale[None, :],
        expand_factor,
        expand_factor.T,
        expand_offset[None, :],
        contract_factor,
        contract_factor.T,
        token_rows,
        emit_projection,
    )

    for group in every_group:
        token_grad = group_sum(token_grad, group)
    token_grad = token_grad.reshape(channels, heads, slices).transpose(1, 2, 0)
    back_num, back_den, asking_slope, lookup_slope, content_slope = token_back(token_grad)
    num_low = block_diagonal(back_num.astype(jnp.bfloat16).transpose(0, 2, 1))
    den_rows = back_den.reshape(lanes, 1)

    everyone = ("head", "pts")
    grads = exchange_sum(grads, everyone)
    grads = gather(grads.astype(jnp.bfloat16), everyone).astype(jnp.float32)

    unit = 2 * channels + 16
    grain = 8 * lax.axis_size("pts")
    block = -(-(local * unit + 8) // grain) * grain
    back_call = pl.pallas_call(
        functools.partial(back_kernel, heads=heads, slices=slices, chunk=256, local=local, block=block),
        grid=(steps,),
        in_specs=[
            row_block,
            row_block,
            whole((total_rows, 2 * width)),
            whole((lanes, width)),
            whole((lanes, 1)),
            whole((lanes, width)),
            whole((heads * channels, total_rows)),
            whole((heads * channels, lanes)),
            whole((heads * channels, width)),
            whole((heads * channels, width)),
            whole((1, width)),
            whole((8, width)),
        ],
        out_specs=whole((groups * block, width)),
        scratch_shapes=[
            pltpu.VMEM((total_rows, tile), jnp.float32),
            pltpu.VMEM((lanes, tile), jnp.float32),
            pltpu.VMEM((heads, tile), jnp.float32),
            pltpu.VMEM((total_rows, tile), jnp.bfloat16),
            pltpu.VMEM((total_rows, width), jnp.float32),
            pltpu.VMEM((lanes, 128), jnp.float32),
            pltpu.VMEM((lanes, 2 * width), jnp.bfloat16),
        ],
        out_shape=jax.ShapeDtypeStruct((groups * block, width), jnp.bfloat16),
        compiler_params=params(),
        cost_estimate=cost(26, rows, width),
        name="back",
    )
    head_grads = back_call(
        scaled,
        back_low,
        pair,
        token_emit,
        den_rows,
        moment,
        energy_rows,
        num_low,
        div_t,
        part_t,
        prefocus_scale[None, :],
        gains,
    )

    head_grads, grads = lax.optimization_barrier((head_grads, grads))
    head_grads = exchange_sum(head_grads, everyone).astype(jnp.bfloat16)
    head_grads = gather(head_grads, ("pts",))
    row = jax.ShapeDtypeStruct((1, width), jnp.float32)
    flat = jax.ShapeDtypeStruct((local * channels, width), jnp.float32)
    divider_slope, partition_slope, energy_slope, sharp_slope, scale_slope, premlp_slope, offset_slope = (
        pl.pallas_call(
            finish_kernel,
            out_shape=[
                flat,
                flat,
                jax.ShapeDtypeStruct((local, channels, slices), jnp.float32),
                jax.ShapeDtypeStruct((1, local * channels), jnp.float32),
                row,
                row,
                row,
            ],
            name="finish",
        )(head_grads)
    )

    def own_heads(value):
        return lax.dynamic_slice_in_dim(value, member * local, local, 0)

    return (
        block_result,
        divider_slope.T,
        partition_slope.T,
        sharp_slope.reshape(-1),
        energy_slope,
        own_heads(asking_slope),
        own_heads(lookup_slope),
        own_heads(content_slope),
        scale_slope.reshape(-1),
        grads[:width],
        premlp_slope.reshape(-1),
        grads[width : 2 * width],
        offset_slope.reshape(-1),
        grads[2 * width : 3 * width],
    )


def solution(mesh):
    in_specs = (
        P("pts", None),
        P(("pts", "head"), None),
        P(None, "head"),
        P(None, "head"),
        P("head"),
        P("head", None, None),
        P("head", None, None),
        P("head", None, None),
        P("head", None, None),
        P(),
        P(),
        P(),
        P(),
        P(),
        P(),
    )
    out_specs = (
        P(("pts", "head"), None),
        P(None, "head"),
        P(None, "head"),
        P("head"),
        P("head", None, None),
        P("head", None, None),
        P("head", None, None),
        P("head", None, None),
        P(),
        P(),
        P(),
        P(),
        P(),
        P(),
    )
    return jax.shard_map(body, mesh=mesh, in_specs=in_specs, out_specs=out_specs, check_vma=False)
```
